32 devices in a mesh: dp: 8 (over z, y), tensor: 4 (over x, core).
Axes of the slice: x: 2, y: 2, z: 4, core: 2. Of those that a mesh axis runs over, the one named last changes fastest.
Arguments:
- layer_input: float32 [4096, 640], P(('dp', 'tensor')), may hold values from -6 to 6
- positions: int32 [4096], P('dp'), may hold values from 0 to 511, as said below
- cotangent: float32 [4096, 640], P(('dp', 'tensor')), may hold values from -12 to 12
- query_weight: float32 [2, 640, 1024], P(None, 'dp', 'tensor'), may hold values from -0.25 to 0.25
- keyval_weight: float32 [2, 640, 512], P(None, 'dp'), may hold values from -0.25 to 0.25
- outproj_weight: float32 [2, 1024, 640], P(None, 'tensor', 'dp'), may hold values from -0.1875 to 0.1875
- gateup_weight: float32 [2, 2, 640, 2048], P(None, None, 'dp', 'tensor'), may hold values from -0.25 to 0.25
- downproj_weight: float32 [2, 2048, 640], P(None, 'tensor', 'dp'), may hold values from -0.125 to 0.125
- gains_weight: float32 [2, 4, 640], P(None, None, 'dp'), may hold values from -0.4 to 0.4
- qkgains_weight: float32 [2, 2, 256], P(None, None, 'dp'), may hold values from -0.4 to 0.4
- query_momentum: float32 [2, 640, 1024], P(None, 'dp', 'tensor'), may hold values from -20 to 20
- keyval_momentum: float32 [2, 640, 512], P(None, 'dp'), may hold values from -20 to 20
- outproj_momentum: float32 [2, 1024, 640], P(None, 'tensor', 'dp'), may hold values from -20 to 20
- gateup_momentum: float32 [2, 2, 640, 2048], P(None, None, 'dp', 'tensor'), may hold values from -20 to 20
- downproj_momentum: float32 [2, 2048, 640], P(None, 'tensor', 'dp'), may hold values from -20 to 20
- gains_momentum: float32 [2, 4, 640], P(None, None, 'dp'), may hold values from -20 to 20
- qkgains_momentum: float32 [2, 2, 256], P(None, None, 'dp'), may hold values from -20 to 20
- query_variance: float32 [2, 640, 1024], P(None, 'dp', 'tensor'), may hold values from 0.12288 to 8.192
- keyval_variance: float32 [2, 640, 512], P(None, 'dp'), may hold values from 0.12288 to 8.192
- outproj_variance: float32 [2, 1024, 640], P(None, 'tensor', 'dp'), may hold values from 0.04096 to 16.384
- gateup_variance: float32 [2, 2, 640, 2048], P(None, None, 'dp', 'tensor'), may hold values from 0.12288 to 8.192
- downproj_variance: float32 [2, 2048, 640], P(None, 'tensor', 'dp'), may hold values from 0.12288 to 8.192
- gains_second_moment: float32 [2, 4, 640], P(None, None, 'dp'), may hold values from 0.12288 to 8.192
- query_key_gains_second_moment: float32 [2, 2, 256], P(None, None, 'dp'), may hold values from 4.096 to 614.4
Outputs:
- layer_output: float32 [4096, 640], P(('dp', 'tensor'))
- input_grad: float32 [4096, 640], P(('dp', 'tensor'))
- gradient_query: float32 [2, 640, 1024], P(None, 'dp', 'tensor')
- gradient_keyval: float32 [2, 640, 512], P(None, 'dp')
- gradient_outproj: float32 [2, 1024, 640], P(None, 'tensor', 'dp')
- gradient_gateup: float32 [2, 2, 640, 2048], P(None, None, 'dp', 'tensor')
- gradient_downproj: float32 [2, 2048, 640], P(None, 'tensor', 'dp')
- gradient_gains: float32 [2, 4, 640], P(None, None, 'dp')
- query_key_gains_gradient: float32 [2, 2, 256], P(None, None, 'dp')
- updated_query: float32 [2, 640, 1024], P(None, 'dp', 'tensor')
- updated_keyval: float32 [2, 640, 512], P(None, 'dp')
- updated_outproj: float32 [2, 1024, 640], P(None, 'tensor', 'dp')
- updated_gateup: float32 [2, 2, 640, 2048], P(None, None, 'dp', 'tensor')
- updated_downproj: float32 [2, 2048, 640], P(None, 'tensor', 'dp')
- updated_gains: float32 [2, 4, 640], P(None, None, 'dp')
- updated_qkgains: float32 [2, 2, 256], P(None, None, 'dp')
- momentum_query: float32 [2, 640, 1024], P(None, 'dp', 'tensor')
- momentum_keyval: float32 [2, 640, 512], P(None, 'dp')
- momentum_outproj: float32 [2, 1024, 640], P(None, 'tensor', 'dp')
- momentum_gateup: float32 [2, 2, 640, 2048], P(None, None, 'dp', 'tensor')
- momentum_downproj: float32 [2, 2048, 640], P(None, 'tensor', 'dp')
- momentum_gains: float32 [2, 4, 640], P(None, None, 'dp')
- momentum_qkgains: float32 [2, 2, 256], P(None, None, 'dp')
- variance_query: float32 [2, 640, 1024], P(None, 'dp', 'tensor')
- variance_keyval: float32 [2, 640, 512], P(None, 'dp')
- variance_outproj: float32 [2, 1024, 640], P(None, 'tensor', 'dp')
- variance_gateup: float32 [2, 2, 640, 2048], P(None, None, 'dp', 'tensor')
- variance_downproj: float32 [2, 2048, 640], P(None, 'tensor', 'dp')
- variance_gains: float32 [2, 4, 640], P(None, None, 'dp')
- variance_qkgains: float32 [2, 2, 256], P(None, None, 'dp')
The draws below stay inside these ranges and needn't reach their ends.
Inputs may be any that keep to these rules, and one draw needn't show every extreme that they name: positions count tokens from the start of their document; each sequence of 512 tokens holds one document or two, the second starting where the position returns to 0; the first sequence of the batch is one document.
All inputs are finite; a program needn't handle non-finite values.
Results may differ from the reference program's by a relative error of at most 0.035.
Values may be sent and summed in bfloat16 or wider, within the bound.
No kernel may reach another device: no remote copies, remote signals or barrier semaphores. Data moves between devices by JAX's collectives and lax.ppermute only.
A program may use at most 128 MiB of HBM per device.

```python
import math
import jax
import jax.numpy as jnp
from jax import lax

D = 640
H = 4
HD = 256
FF = 2048
SEQ = 512
WINDOW = 256
TOKENS = 4096


def draw_positions(key, part):
    count = TOKENS // SEQ
    cuts = jax.random.randint(key, (count,), 0, SEQ, dtype=jnp.int32)
    cuts = jnp.where(jnp.arange(count, dtype=jnp.int32) == 0, 0, cuts)
    where_at = jnp.arange(TOKENS, dtype=jnp.int32) % SEQ
    split_per_shard = jnp.repeat(cuts, SEQ, total_repeat_length=TOKENS)
    return jnp.where(where_at >= split_per_shard, where_at - split_per_shard, where_at).astype(jnp.int32)


def draw_query_key_gains_second_moment(key, part):
    unit = jax.random.uniform(key, (2, 2, HD), jnp.float32)
    lower = 0.001 * TOKENS
    upper = 0.06 * TOKENS
    spread = math.log(upper / lower)
    return (lower * jnp.exp(unit * spread)).astype(jnp.float32)


def spiked(drawn, own_key, source, target, shards_of, factor):
    def block_of(axis_at):
        return (jnp.arange(drawn.shape[axis_at]) // (drawn.shape[axis_at] // shards_of)).reshape((-1,) + (1,) * (drawn.ndim - 1 - axis_at))

    one_side = jax.random.permutation(own_key, shards_of)[block_of(target)]
    far = (block_of(target) + shards_of // 2) % shards_of
    return jnp.where((block_of(source) == one_side) | (block_of(source) == far), factor * drawn, drawn)


def steps_of(rng, extent, cuts, smallest, largest):
    def one(dim, blocks):
        heights = jax.random.uniform(jax.random.fold_in(jax.random.fold_in(rng, 6), dim), (blocks,), jnp.float32, smallest / len(cuts), largest / len(cuts))
        return jnp.repeat(jnp.exp(heights), extent[dim] // blocks).reshape((-1,) + (1,) * (len(extent) - dim - 1))

    level = one(*cuts[0])
    for cut in cuts[1:]:
        level = level * one(*cut)
    return level


def centred(own_key, shape, scale, limit, split=(), held_as=jnp.bfloat16):
    factor_of = steps_of(own_key, shape, split, -0.22, 0.18) if split else 1.0
    array = jax.random.normal(own_key, shape, jnp.float32) * scale * factor_of
    return jnp.minimum(jnp.maximum(array, -limit), limit).astype(held_as)


def bell_draw_with(rng, extent, scale, bound, shards, heavy, held_as=jnp.bfloat16):
    array = scale * jax.random.normal(rng, extent, jnp.float32)
    if shards:
        array = array * steps_of(rng, extent, shards, -0.22, 0.18)
    return jnp.clip(spiked(array, jax.random.fold_in(rng, 3), *heavy), -bound, bound).astype(held_as)


def setup_inputs(seed: int = 0) -> dict:
    keys = jax.random.split(jax.random.key(seed), 25)
    layer_input = centred(keys[0], (TOKENS, D), 1.0, 6.0, ((0, 32),), jnp.float32)
    positions = draw_positions(jax.random.fold_in(keys[24], 71), 0)
    cotangent = bell_draw_with(keys[2], (TOKENS, D), 1.0, 12.0, ((0, 32),), (0, 1, 32, 2.75), jnp.float32)
    query_weight = centred(keys[3], (2, D, H * HD), D ** -0.5, 0.25, ((1, 8), (2, 4)), jnp.float32)
    keyval_weight = centred(keys[4], (2, D, 2 * HD), D ** -0.5, 0.25, ((1, 8),), jnp.float32)
    outproj_weight = centred(keys[5], (2, H * HD, D), (H * HD) ** -0.5, 0.1875, ((1, 4), (2, 8)), jnp.float32)
    gateup_weight = centred(keys[6], (2, 2, D, FF), D ** -0.5, 0.25, ((2, 8), (3, 4)), jnp.float32)
    downproj_weight = centred(keys[7], (2, FF, D), FF ** -0.5, 0.125, ((1, 4), (2, 8)), jnp.float32)
    gains_weight = jnp.clip(jax.random.uniform(keys[8], (2, 4, D), jnp.float32, -0.4, 0.4) * steps_of(keys[8], (2, 4, D), ((2, 8),), -0.4, 0.0), -0.4, 0.4)
    qkgains_weight = jnp.clip(jax.random.uniform(keys[9], (2, 2, HD), jnp.float32, -0.4, 0.4) * steps_of(keys[9], (2, 2, HD), ((2, 8),), -0.4, 0.0), -0.4, 0.4)
    query_momentum = centred(keys[10], (2, D, H * HD), (0.05 * TOKENS ** 0.5), 20.0, ((1, 8), (2, 4)), jnp.float32)
    keyval_momentum = centred(keys[11], (2, D, 2 * HD), (0.05 * TOKENS ** 0.5), 20.0, ((1, 8),), jnp.float32)
    outproj_momentum = centred(keys[12], (2, H * HD, D), (0.05 * TOKENS ** 0.5), 20.0, ((1, 4), (2, 8)), jnp.float32)
    gateup_momentum = centred(keys[13], (2, 2, D, FF), (0.05 * TOKENS ** 0.5), 20.0, ((2, 8), (3, 4)), jnp.float32)
    downproj_momentum = centred(keys[14], (2, FF, D), (0.05 * TOKENS ** 0.5), 20.0, ((1, 4), (2, 8)), jnp.float32)
    gains_momentum = centred(keys[15], (2, 4, D), (0.05 * TOKENS ** 0.5), 20.0, ((2, 8),), jnp.float32)
    qkgains_momentum = centred(keys[16], (2, 2, HD), (0.05 * TOKENS ** 0.5), 20.0, ((2, 8),), jnp.float32)
    query_variance = jnp.clip(jnp.exp(math.log(8.192) - 4.199705 * jax.random.uniform(keys[17], (2, D, H * HD), jnp.float32) ** steps_of(keys[17], (2, D, H * HD), ((1, 8), (2, 4)), -0.2, 0.2)), 0.12288, 8.192)
    keyval_variance = jnp.clip(jnp.exp(math.log(8.192) - 4.199705 * jax.random.uniform(keys[18], (2, D, 2 * HD), jnp.float32) ** steps_of(keys[18], (2, D, 2 * HD), ((1, 8),), -0.2, 0.2)), 0.12288, 8.192)
    outproj_variance = jnp.clip(jnp.exp(math.log(16.384) - 5.9914646 * jax.random.uniform(keys[19], (2, H * HD, D), jnp.float32) ** steps_of(keys[19], (2, H * HD, D), ((1, 4), (2, 8)), -0.2, 0.2)), 0.04096, 16.384)
    gateup_variance = jnp.clip(jnp.exp(math.log(8.192) - 4.199705 * jax.random.uniform(keys[20], (2, 2, D, FF), jnp.float32) ** steps_of(keys[20], (2, 2, D, FF), ((2, 8), (3, 4)), -0.2, 0.2)), 0.12288, 8.192)
    downproj_variance = jnp.clip(jnp.exp(math.log(8.192) - 4.199705 * jax.random.uniform(keys[21], (2, FF, D), jnp.float32) ** steps_of(keys[21], (2, FF, D), ((1, 4), (2, 8)), -0.2, 0.2)), 0.12288, 8.192)
    gains_second_moment = jnp.clip(jnp.exp(math.log(8.192) - 4.199705 * jax.random.uniform(keys[22], (2, 4, D), jnp.float32) ** steps_of(keys[22], (2, 4, D), ((2, 8),), -0.2, 0.2)), 0.12288, 8.192)
    query_key_gains_second_moment = draw_query_key_gains_second_moment(jax.random.fold_in(keys[24], 71), 0)
    return dict(layer_input=layer_input, positions=positions, cotangent=cotangent, query_weight=query_weight, keyval_weight=keyval_weight, outproj_weight=outproj_weight, gateup_weight=gateup_weight, downproj_weight=downproj_weight, gains_weight=gains_weight, qkgains_weight=qkgains_weight, query_momentum=query_momentum, keyval_momentum=keyval_momentum, outproj_momentum=outproj_momentum, gateup_momentum=gateup_momentum, downproj_momentum=downproj_momentum, gains_momentum=gains_momentum, qkgains_momentum=qkgains_momentum, query_variance=query_variance, keyval_variance=keyval_variance, outproj_variance=outproj_variance, gateup_variance=gateup_variance, downproj_variance=downproj_variance, gains_second_moment=gains_second_moment, query_key_gains_second_moment=query_key_gains_second_moment)


norm_eps = 1e-06
rope_bases = (10000.0, 1000000.0)
learn_rate = 0.02
beta_first = 0.9
beta_second = 0.999
adam_eps = 1e-08
decay_rate = 0.1
adam_step = 4.0
masked_value = -1e+30

def rms_scale(values, gain):
    mean_sq = lax.optimization_barrier(jnp.mean(values * values, axis=-1, keepdims=True))
    return values * lax.rsqrt(mean_sq + norm_eps) * (1.0 + gain)

def rotary(values, places, base):
    width = values.shape[-1]
    half = width // 2
    expo = jnp.arange(half, dtype=jnp.float32) * (2.0 / width)
    freqs = jnp.exp(-expo * jnp.log(jnp.float32(base)))
    angles = places.astype(jnp.float32)[:, None, None] * freqs[None, None, :]
    cosine = jnp.cos(angles)
    sine = jnp.sin(angles)
    first = values[..., :half]
    second = values[..., half:]
    return jnp.concatenate([first * cosine - second * sine, second * cosine + first * sine], axis=-1)

def query_key(query_raw, key_raw, qk_gain, places, base):
    query_rot = rotary(rms_scale(query_raw, qk_gain[0]), places, base)
    key_rot = rotary(rms_scale(key_raw, qk_gain[1]), places, base)
    return (query_rot, key_rot)

def gated(gate, up):
    return jax.nn.gelu(gate, approximate=True) * up

def rounded(values):
    return lax.optimization_barrier(values.astype(jnp.bfloat16)).astype(jnp.float32)

def visible(offsets, window):
    length = offsets.shape[0]
    where_at = jnp.arange(length, dtype=jnp.int32)
    gap = where_at[:, None] - where_at[None, :]
    return (gap >= 0) & (gap < window) & (offsets[:, None] == offsets[None, :])

def scores_of(query_low, key_low, allowed):
    scale = query_low.shape[-1] ** (-0.5)
    scores = jnp.einsum('qhd,kd->hqk', query_low.astype(jnp.float32), key_low.astype(jnp.float32)) * scale
    return jnp.where(allowed[None], scores, masked_value)

def attend_forward(query_low, key_low, value_low, allowed):
    scores = scores_of(query_low, key_low, allowed)
    peak = lax.optimization_barrier(jnp.max(scores, axis=-1, keepdims=True))
    logsum = peak + jnp.log(lax.optimization_barrier(jnp.sum(jnp.exp(scores - peak), axis=-1, keepdims=True)))
    probs_low = jnp.exp(scores - logsum).astype(jnp.bfloat16)
    mixed = jnp.einsum('hqk,kd->qhd', probs_low.astype(jnp.float32), value_low.astype(jnp.float32))
    return (mixed.astype(jnp.bfloat16), logsum[..., 0])

def attend_backward(query_low, key_low, value_low, logsum, back_mixed, allowed):
    scale = query_low.shape[-1] ** (-0.5)
    scores = scores_of(query_low, key_low, allowed)
    probs = jnp.exp(scores - logsum[..., None])
    back_probs = jnp.einsum('qhd,kd->hqk', back_mixed.astype(jnp.float32), value_low.astype(jnp.float32))
    delta = lax.optimization_barrier(jnp.sum(probs * back_probs, axis=-1, keepdims=True))
    back_scores = (probs * (back_probs - delta) * scale).astype(jnp.bfloat16).astype(jnp.float32)
    back_query = jnp.einsum('hqk,kd->qhd', back_scores, key_low.astype(jnp.float32))
    back_key = jnp.einsum('hqk,qhd->khd', back_scores, query_low.astype(jnp.float32))
    probs_low = probs.astype(jnp.bfloat16).astype(jnp.float32)
    back_value = jnp.einsum('hqk,qhd->khd', probs_low, back_mixed.astype(jnp.float32))
    return (back_query, back_key, back_value)

def layer_forward(x_in, places, allowed, weights, base):
    w_query, w_keyval, w_outproj, w_gateup, w_downproj, gain_rows, qk_gain = weights
    width = qk_gain.shape[-1]
    heads = w_query.shape[1] // width
    length = x_in.shape[0]
    norm_one = rms_scale(x_in, gain_rows[0]).astype(jnp.bfloat16)
    query_raw = jnp.dot(norm_one, w_query, preferred_element_type=jnp.float32).reshape(length, heads, width)
    keyval_raw = jnp.dot(norm_one, w_keyval, preferred_element_type=jnp.float32)
    query_rot, key_rot = query_key(query_raw, keyval_raw[:, None, :width], qk_gain, places, base)
    query_low = query_rot.astype(jnp.bfloat16)
    key_low = key_rot[:, 0].astype(jnp.bfloat16)
    value_low = keyval_raw[:, width:].astype(jnp.bfloat16)
    mixed, logsum = attend_forward(query_low, key_low, value_low, allowed)
    attn_flat = mixed.reshape(length, heads * width)
    z_one = jnp.dot(attn_flat, w_outproj, preferred_element_type=jnp.float32)
    hidden = x_in + rms_scale(z_one, gain_rows[1])
    norm_three = rms_scale(hidden, gain_rows[2]).astype(jnp.bfloat16)
    gate = jnp.dot(norm_three, w_gateup[0], preferred_element_type=jnp.float32)
    up = jnp.dot(norm_three, w_gateup[1], preferred_element_type=jnp.float32)
    act = gated(gate, up).astype(jnp.bfloat16)
    z_two = jnp.dot(act, w_downproj, preferred_element_type=jnp.float32)
    result = hidden + rms_scale(z_two, gain_rows[3])
    saved = (norm_one, query_raw, keyval_raw, query_low, key_low, value_low, attn_flat, logsum, z_one, hidden, norm_three, gate, up, act, z_two)
    return (result, saved)

def layer_backward(x_in, places, allowed, weights, base, saved, back_out):
    w_query, w_keyval, w_outproj, w_gateup, w_downproj, gain_rows, qk_gain = weights
    norm_one, query_raw, keyval_raw, query_low, key_low, value_low, attn_flat, logsum, z_one, hidden, norm_three, gate, up, act, z_two = saved
    width = qk_gain.shape[-1]
    heads = w_query.shape[1] // width
    length = x_in.shape[0]
    back_ztwo, grad_three = jax.vjp(rms_scale, z_two, gain_rows[3])[1](back_out)
    ztwo_low = back_ztwo.astype(jnp.bfloat16)
    back_act = jnp.dot(ztwo_low, w_downproj.T, preferred_element_type=jnp.float32)
    grad_down = jnp.dot(act.T, ztwo_low, preferred_element_type=jnp.float32)
    back_gate, back_up = jax.vjp(gated, gate, up)[1](back_act)
    gate_low = back_gate.astype(jnp.bfloat16)
    up_low = back_up.astype(jnp.bfloat16)
    grad_gateup = jnp.stack([jnp.dot(norm_three.T, gate_low, preferred_element_type=jnp.float32), jnp.dot(norm_three.T, up_low, preferred_element_type=jnp.float32)])
    back_three = jnp.dot(gate_low, w_gateup[0].T, preferred_element_type=jnp.float32) + jnp.dot(up_low, w_gateup[1].T, preferred_element_type=jnp.float32)
    back_hnorm, gradient_second_layer = jax.vjp(rms_scale, hidden, gain_rows[2])[1](back_three)
    back_hidden = back_out + back_hnorm
    back_zone, grad_one = jax.vjp(rms_scale, z_one, gain_rows[1])[1](back_hidden)
    zone_low = back_zone.astype(jnp.bfloat16)
    back_attn = jnp.dot(zone_low, w_outproj.T, preferred_element_type=jnp.float32).astype(jnp.bfloat16)
    grad_outproj = jnp.dot(attn_flat.T, zone_low, preferred_element_type=jnp.float32)
    back_query, back_key, back_value = attend_backward(query_low, key_low, value_low, logsum, back_attn.reshape(length, heads, width), allowed)
    key_rep = jnp.broadcast_to(keyval_raw[:, None, :width], (length, heads, width))

    def rotate_both(query_part, key_part, gain_part):
        return query_key(query_part, key_part, gain_part, places, base)
    back_qraw, back_kraw, grad_qk = jax.vjp(rotate_both, query_raw, key_rep, qk_gain)[1]((back_query, back_key))
    query_back_low = back_qraw.reshape(length, heads * width).astype(jnp.bfloat16)
    keyval_back_low = jnp.concatenate([back_kraw, back_value], axis=-1).astype(jnp.bfloat16)
    grad_query = jnp.dot(norm_one.T, query_back_low, preferred_element_type=jnp.float32)
    grad_keyval = jnp.einsum('gd,ghc->dc', norm_one.astype(jnp.float32), keyval_back_low.astype(jnp.float32))
    back_one = jnp.dot(query_back_low, w_query.T, preferred_element_type=jnp.float32) + jnp.einsum('ghc,dc->gd', keyval_back_low.astype(jnp.float32), w_keyval.astype(jnp.float32))
    back_xnorm, grad_zero = jax.vjp(rms_scale, x_in, gain_rows[0])[1](back_one)
    back_in = back_hidden + back_xnorm
    grads = (grad_query, grad_keyval, grad_outproj, grad_gateup, grad_down, jnp.stack([grad_zero, grad_one, gradient_second_layer, grad_three]), grad_qk)
    return (back_in, grads)

def adamw(param, grad, moment, second):
    moment_new = beta_first * moment + (1.0 - beta_first) * grad
    second_new = beta_second * second + (1.0 - beta_second) * grad * grad
    moment_hat = moment_new / (1.0 - beta_first ** adam_step)
    second_hat = second_new / (1.0 - beta_second ** adam_step)
    updated = param - learn_rate * (moment_hat / (jnp.sqrt(second_hat) + adam_eps) + decay_rate * param)
    return (updated, moment_new, second_new)

def reference(layer_input, positions, cotangent, query_weight, keyval_weight, outproj_weight, gateup_weight, downproj_weight, gains_weight, qkgains_weight, query_momentum, keyval_momentum, outproj_momentum, gateup_momentum, downproj_momentum, gains_momentum, qkgains_momentum, query_variance, keyval_variance, outproj_variance, gateup_variance, downproj_variance, gains_second_moment, query_key_gains_second_moment):
    params = (query_weight, keyval_weight, outproj_weight, gateup_weight, downproj_weight, gains_weight, qkgains_weight)
    momenta = (query_momentum, keyval_momentum, outproj_momentum, gateup_momentum, downproj_momentum, gains_momentum, qkgains_momentum)
    seconds = (query_variance, keyval_variance, outproj_variance, gateup_variance, downproj_variance, gains_second_moment, query_key_gains_second_moment)
    layers = []
    for depth_level_index in range(2):
        mats = tuple((param[depth_level_index].astype(jnp.bfloat16) for param in params[:5]))
        gains = tuple((rounded(param[depth_level_index]) for param in params[5:]))
        layers.append(mats + gains)
    windows = (WINDOW, SEQ)
    where_at = jnp.arange(SEQ, dtype=jnp.int32)
    count = TOKENS // SEQ

    def one_sequence(carry, items):
        x_seq, place_seq, back_seq = items
        offsets = place_seq - where_at
        masks = [visible(offsets, windows[0]), visible(offsets, windows[1])]
        middle, saved_zero = layer_forward(x_seq, place_seq, masks[0], layers[0], rope_bases[0])
        top, saved_one = layer_forward(middle, place_seq, masks[1], layers[1], rope_bases[1])
        back_middle, grads_one = layer_backward(middle, place_seq, masks[1], layers[1], rope_bases[1], saved_one, back_seq)
        back_in, grads_zero = layer_backward(x_seq, place_seq, masks[0], layers[0], rope_bases[0], saved_zero, back_middle)
        summed = tuple((total + jnp.stack([first, second]) for total, first, second in zip(carry, grads_zero, grads_one)))
        return (summed, (top, back_in))
    init = tuple((jnp.zeros(param.shape, jnp.float32) for param in params))
    gradients, (tops, backs) = lax.scan(one_sequence, init, (layer_input.reshape(count, SEQ, D), positions.reshape(count, SEQ), cotangent.reshape(count, SEQ, D)))
    results = [adamw(param, grad, moment, second) for param, grad, moment, second in zip(params, gradients, momenta, seconds)]
    return (tops.reshape(TOKENS, D), backs.reshape(TOKENS, D), gradients[0], gradients[1], gradients[2], gradients[3], gradients[4], gradients[5], gradients[6], results[0][0], results[1][0], results[2][0], results[3][0], results[4][0], results[5][0], results[6][0], results[0][1], results[1][1], results[2][1], results[3][1], results[4][1], results[5][1], results[6][1], results[0][2], results[1][2], results[2][2], results[3][2], results[4][2], results[5][2], results[6][2])
```

```python
import jax
import jax.numpy as jnp
from jax import lax
from jax.sharding import PartitionSpec as P

SEQ = 512
WINDOW = 256


norm_eps = 1e-06
rope_bases = (10000.0, 1000000.0)
learn_rate = 0.02
beta_first = 0.9
beta_second = 0.999
adam_eps = 1e-08
decay_rate = 0.1
adam_step = 4.0
masked_value = -1e30

low = jnp.bfloat16
full = jnp.float32

CORE_PAIRS = [(0, 1), (1, 0), (2, 3), (3, 2)]
CHIP_PAIRS = [(0, 2), (2, 0), (1, 3), (3, 1)]
CYCLE = (0, 2, 4, 6, 7, 5, 3, 1)
PLACE = (0, 7, 1, 6, 2, 5, 3, 4)
EXTRA = 128


def dot(left, right, dims):
    return lax.dot_general(left, right, (dims, ((), ())), preferred_element_type=full)


def rms_scale(values, gain):
    mean_sq = jnp.mean(values * values, axis=-1, keepdims=True)
    return values * lax.rsqrt(mean_sq + norm_eps) * (1.0 + gain)


def gated(gate, up):
    return jax.nn.gelu(gate, approximate=True) * up


def rotate(values, table):
    cosine, sine = table
    half = values.shape[-1] // 2
    first = values[..., :half]
    second = values[..., half:]
    return jnp.concatenate(
        [first * cosine - second * sine, second * cosine + first * sine], axis=-1
    )


def rotary_table(places, width, base):
    half = width // 2
    expo = jnp.arange(half, dtype=full) * (2.0 / width)
    freqs = jnp.exp(-expo * jnp.log(full(base)))
    angles = places.astype(full)[:, None] * freqs[None, :]
    return (jnp.cos(angles), jnp.sin(angles))


def tuned(mesh_sizes):
    return mesh_sizes == (8, 4)


def turn(step):
    count = len(CYCLE)
    return [(CYCLE[i], CYCLE[(i + step) % count]) for i in range(count)]


def at_cycle(position):
    place = jnp.asarray(CYCLE, jnp.int32)
    return place[position % len(CYCLE)]


def my_place():
    return jnp.asarray(PLACE, jnp.int32)[lax.axis_index("dp")]


def ring_gather(block):
    rows = block.shape[0]
    count = len(CYCLE)
    mine = my_place()
    out = jnp.zeros((count * rows, block.shape[1]), block.dtype)

    def put(out, piece, position):
        return lax.dynamic_update_slice(out, piece, (at_cycle(position) * rows, 0))

    out = put(out, block, mine)
    ahead = behind = block
    for step in range(1, count // 2 + 1):
        ahead = lax.ppermute(ahead, "dp", turn(1))
        out = put(out, ahead, mine + count - step)
        if step < count // 2:
            behind = lax.ppermute(behind, "dp", turn(-1))
            out = put(out, behind, mine + step)
    return out


def ring_scatter(terms):
    count = len(CYCLE)
    rows = terms.shape[0] // count
    mine = my_place()

    def take(position):
        return lax.dynamic_slice(
            terms, (at_cycle(position) * rows, 0), (rows, terms.shape[1])
        ).astype(full)

    half = count // 2
    ahead = take(mine + half)
    behind = take(mine + count - half + 1)
    for step in range(1, half + 1):
        ahead = lax.ppermute(ahead.astype(low), "dp", turn(1)).astype(full)
        if step < half:
            ahead = ahead + take(mine + half - step)
        if step < half:
            behind = lax.ppermute(behind.astype(low), "dp", turn(-1)).astype(full)
            if step < half - 1:
                behind = behind + take(mine + count - half + 1 + step)
    return ahead + behind + take(mine)


def gather_native(block):
    return lax.all_gather(block, "dp", axis=0, tiled=True)


def scatter_native(terms):
    return lax.psum_scatter(terms, "dp", scatter_dimension=0, tiled=True).astype(full)


class Pairs:
    def __init__(self, group):
        self.quarter = group // 4
        self.me = lax.axis_index("tensor")
        self.core = self.me % 2
        self.chip = self.me // 2
        self.group = group
        self.weight = 0.5

    def own_rows(self, values):
        other = lax.ppermute(values, "tensor", CHIP_PAIRS)
        first = jnp.where(self.chip == 0, values, other)
        second = jnp.where(self.chip == 0, other, values)
        return jnp.concatenate([first, second], axis=0)

    def my_rows(self, owned):
        return lax.dynamic_slice_in_dim(owned, self.chip * self.quarter, self.quarter, 0)

    def order(self):
        step = jnp.arange(self.quarter, dtype=jnp.int32)
        starts = (self.core, 2 + self.core, 1 - self.core, 3 - self.core)
        return jnp.concatenate([start * self.quarter + step for start in starts])

    def arrange(self, values):
        parts = [values[i * self.quarter : (i + 1) * self.quarter] for i in range(4)]
        swapped = jnp.concatenate([parts[1], parts[3], parts[0], parts[2]])
        return jnp.where(
            self.core == 0, jnp.concatenate([parts[0], parts[2], parts[1], parts[3]]), swapped
        )

    def spread(self, owned):
        return jnp.concatenate([owned, lax.ppermute(owned, "tensor", CORE_PAIRS)], axis=0)

    def total(self, partial):
        half = 2 * self.quarter
        pair = partial[:half] + lax.ppermute(
            partial[half:].astype(low), "tensor", CORE_PAIRS
        ).astype(full)
        return pair + lax.ppermute(pair.astype(low), "tensor", CHIP_PAIRS).astype(full)

    def everywhere(self, values):
        pair = values + lax.ppermute(values.astype(low), "tensor", CORE_PAIRS).astype(full)
        return pair + lax.ppermute(pair.astype(low), "tensor", CHIP_PAIRS).astype(full)


class Plain:
    def __init__(self, group):
        self.group = group
        self.weight = 1.0

    def own_rows(self, values):
        return values

    def my_rows(self, owned):
        return owned

    def order(self):
        return jnp.arange(self.group, dtype=jnp.int32)

    def arrange(self, values):
        return values

    def spread(self, owned):
        return lax.all_gather(owned, "tensor", axis=0, tiled=True)

    def total(self, partial):
        return lax.psum_scatter(
            partial.astype(low), "tensor", scatter_dimension=0, tiled=True
        ).astype(full)

    def everywhere(self, values):
        return lax.psum(values.astype(low), "tensor").astype(full)


def pad_rows(values, rows):
    return jnp.pad(values, ((0, rows - values.shape[0]), (0, 0)))


def pack_layer(params, level):
    query, keyval, outproj, gateup, down, gains, qk_gains = (
        param[level].astype(low) for param in params
    )
    rows = query.shape[0]
    extra = jnp.concatenate([gains.T, pad_rows(qk_gains.T, rows)], axis=1)
    extra = jnp.pad(extra, ((0, 0), (0, EXTRA - extra.shape[1])))
    first = jnp.concatenate([query, keyval, extra], axis=1)
    second = jnp.concatenate([outproj.T, gateup[0], gateup[1], down.T], axis=1)
    return first, second


def unpack_extra(extra, count_norms, width, dp):
    gains = extra[:, :count_norms].astype(full).T
    rows = extra.shape[0] // dp
    qk = extra[:, count_norms : count_norms + 2].reshape(dp, rows, 2)[:, : width // dp]
    return gains, qk.reshape(width, 2).astype(full).T


def pack_extra(gains, qk, dp):
    width = qk.shape[1]
    rows = gains.shape[1] // dp
    spread = jnp.pad(qk.T.reshape(dp, width // dp, 2), ((0, 0), (0, rows - width // dp), (0, 0)))
    extra = jnp.concatenate([gains.T, spread.reshape(dp * rows, 2)], axis=1)
    return jnp.pad(extra, ((0, 0), (0, EXTRA - extra.shape[1]))).astype(low)


def split_first(first, heads_width, width):
    a = heads_width
    return first[:, :a], first[:, a : a + 2 * width], first[:, a + 2 * width :]


def split_second(second, heads_width, hidden):
    a = heads_width
    return second[:, :a], second[:, a : a + 2 * hidden], second[:, a + 2 * hidden :]


def heads_of(values, width):
    return values.reshape(values.shape[0], values.shape[1] // width, width)


def scores_of(query_low, key_low, allowed):
    scale = query_low.shape[-1] ** (-0.5)
    scores = jnp.einsum("qhd,kd->hqk", query_low, key_low, preferred_element_type=full) * scale
    return jnp.where(allowed[None], scores, masked_value)


def attend_forward(query_low, key_low, value_low, allowed):
    scores = scores_of(query_low, key_low, allowed)
    peak = jnp.max(scores, axis=-1, keepdims=True)
    logsum = peak + jnp.log(jnp.sum(jnp.exp(scores - peak), axis=-1, keepdims=True))
    probs_low = jnp.exp(scores - logsum).astype(low)
    mixed = jnp.einsum("hqk,kd->qhd", probs_low, value_low, preferred_element_type=full)
    return mixed.astype(low), logsum


def attend_backward(query_low, key_low, value_low, logsum, back_mixed, allowed):
    scale = query_low.shape[-1] ** (-0.5)
    scores = scores_of(query_low, key_low, allowed)
    probs = jnp.exp(scores - logsum)
    back_probs = jnp.einsum("qhd,kd->hqk", back_mixed, value_low, preferred_element_type=full)
    delta = jnp.sum(probs * back_probs, axis=-1, keepdims=True)
    back_scores = (probs * (back_probs - delta) * scale).astype(low)
    back_query = jnp.einsum("hqk,kd->qhd", back_scores, key_low, preferred_element_type=full)
    back_key = jnp.einsum("hqk,qhd->khd", back_scores, query_low, preferred_element_type=full)
    probs_low = probs.astype(low)
    back_value = jnp.einsum("hqk,qhd->khd", probs_low, back_mixed, preferred_element_type=full)
    return back_query, back_key, back_value


def query_key(query_raw, key_raw, qk_gain, table):
    return (
        rotate(rms_scale(query_raw, qk_gain[0]), table),
        rotate(rms_scale(key_raw, qk_gain[1]), table),
    )


def forward_layer(x_own, norm_one, weights, gain_rows, qk_gain, allowed, table, moves):
    w_query, w_keyval, w_outproj, w_gateup, w_down = weights
    width = qk_gain.shape[-1]
    query_raw = heads_of(dot(norm_one, w_query, ((1,), (0,))), width)
    keyval_raw = dot(norm_one, w_keyval, ((1,), (0,)))
    query_rot, key_rot = query_key(query_raw, keyval_raw[:, None, :width], qk_gain, table)
    query_low = query_rot.astype(low)
    key_low = key_rot[:, 0].astype(low)
    value_low = keyval_raw[:, width:].astype(low)
    mixed, logsum = attend_forward(query_low, key_low, value_low, allowed)
    attn_flat = mixed.reshape(mixed.shape[0], -1)
    z_one = moves.total(dot(attn_flat, w_outproj, ((1,), (1,))))
    hidden = x_own + rms_scale(z_one, gain_rows[1])
    norm_three = moves.spread(rms_scale(hidden, gain_rows[2]).astype(low))
    both = dot(norm_three, w_gateup, ((1,), (0,)))
    half = both.shape[1] // 2
    act = gated(both[:, :half], both[:, half:]).astype(low)
    z_two = moves.total(dot(act, w_down, ((1,), (1,))))
    result = hidden + rms_scale(z_two, gain_rows[3])
    saved = (
        norm_one, query_raw, keyval_raw, query_low, key_low, value_low, attn_flat, logsum,
        z_one, hidden, norm_three, both, act, z_two,
    )
    return result, saved


def backward_ffn(weights, gain_rows, saved, back_out, moves):
    z_one, hidden, norm_three, both, act, z_two = saved[8:]
    w_outproj, w_gateup, w_down = weights[2:]
    half = both.shape[1] // 2
    back_ztwo, grad_three = jax.vjp(rms_scale, z_two, gain_rows[3])[1](back_out)
    ztwo_low = moves.spread(back_ztwo.astype(low))
    back_act = dot(ztwo_low, w_down, ((1,), (0,)))
    back_gate, back_up = jax.vjp(gated, both[:, :half], both[:, half:])[1](back_act)
    both_low = jnp.concatenate([back_gate.astype(low), back_up.astype(low)], axis=1)
    back_three = moves.total(dot(both_low, w_gateup, ((1,), (1,))))
    grad_gateup = dot(norm_three, both_low, ((0,), (0,))).astype(low)
    grad_down = dot(ztwo_low, act, ((0,), (0,))).astype(low)
    back_hnorm, grad_two = jax.vjp(rms_scale, hidden, gain_rows[2])[1](back_three)
    back_hidden = back_out + back_hnorm
    back_zone, grad_one = jax.vjp(rms_scale, z_one, gain_rows[1])[1](back_hidden)
    return back_hidden, back_zone, (grad_gateup, grad_down), (grad_one, grad_two, grad_three)


def backward_attention(x_own, weights, gain_rows, qk_gain, saved, back_hidden, back_zone, allowed, table, moves):
    norm_one, query_raw, keyval_raw, query_low, key_low, value_low, attn_flat, logsum = saved[:8]
    w_query, w_keyval, w_outproj = weights[:3]
    width = qk_gain.shape[-1]
    group = norm_one.shape[0]
    heads = query_low.shape[1]
    zone_low = moves.spread(back_zone.astype(low))
    back_attn = dot(zone_low, w_outproj, ((1,), (0,))).astype(low)
    grad_outproj = dot(zone_low, attn_flat, ((0,), (0,))).astype(low)
    back_query, back_key, back_value = attend_backward(
        query_low, key_low, value_low, logsum, heads_of(back_attn, width), allowed
    )
    key_rep = jnp.broadcast_to(keyval_raw[:, None, :width], (group, heads, width))

    def rotate_both(query_part, key_part, gain_part):
        return query_key(query_part, key_part, gain_part, table)

    back_qraw, back_kraw, grad_qk = jax.vjp(rotate_both, query_raw, key_rep, qk_gain)[1](
        (back_query, back_key)
    )
    query_back = back_qraw.reshape(group, -1).astype(low)
    keyval_back = jnp.concatenate([back_kraw, back_value], axis=-1).astype(low)
    if heads == 1:
        keyval_back = keyval_back[:, 0]
        both = jnp.concatenate([query_back, keyval_back], axis=1)
        w_both = jnp.concatenate([w_query, w_keyval], axis=1)
        back_one = dot(both, w_both, ((1,), (1,)))
        grad_both = dot(norm_one, both, ((0,), (0,))).astype(low)
    else:
        back_one = dot(query_back, w_query, ((1,), (1,))) + jnp.einsum(
            "ghc,dc->gd", keyval_back, w_keyval, preferred_element_type=full
        )
        grad_keyval = jnp.einsum("gd,ghc->dc", norm_one, keyval_back, preferred_element_type=full)
        grad_query = dot(norm_one, query_back, ((0,), (0,)))
        grad_both = jnp.concatenate([grad_query, grad_keyval], axis=1).astype(low)
    back_one = moves.total(back_one)
    back_xnorm, grad_zero = jax.vjp(rms_scale, x_own, gain_rows[0])[1](back_one)
    return back_hidden + back_xnorm, grad_both, grad_outproj, grad_zero, grad_qk


def adamw(param, grad, moment, second):
    moment_new = beta_first * moment + (1.0 - beta_first) * grad
    second_new = beta_second * second + (1.0 - beta_second) * grad * grad
    moment_hat = moment_new / (1.0 - beta_first**adam_step)
    second_hat = second_new / (1.0 - beta_second**adam_step)
    updated = param - learn_rate * (
        moment_hat / (jnp.sqrt(second_hat) + adam_eps) + decay_rate * param
    )
    return (updated, moment_new, second_new)


def on_device(layer_input, positions, cotangent, *state):
    params, momenta, seconds = state[:7], state[7:14], state[14:]
    dp = lax.axis_size("dp")
    fast = tuned((dp, lax.axis_size("tensor")))
    group = positions.shape[0]
    heads_width = params[0].shape[2]
    hidden_width = params[3].shape[3]
    count_norms = params[5].shape[1]
    width = params[6].shape[2] * dp
    moves = Pairs(group) if fast else Plain(group)
    first_gather = ring_gather if fast else gather_native
    last_scatter = ring_scatter if fast else scatter_native

    packs = [pack_layer(params, level) for level in range(2)]
    firsts = [first_gather(packs[0][0])]
    rest = gather_native(packs[0][1])
    seconds_low = [rest]
    later = gather_native(jnp.concatenate(packs[1], axis=1))
    firsts.append(later[:, : packs[1][0].shape[1]])
    seconds_low.append(later[:, packs[1][0].shape[1] :])

    where_at = moves.order()
    places = moves.arrange(positions)
    offsets = places - where_at % SEQ
    gap = where_at[:, None] - where_at[None, :]
    together = (gap >= 0) & (offsets[:, None] == offsets[None, :])
    if group > SEQ:
        together = together & (where_at[:, None] // SEQ == where_at[None, :] // SEQ)
    masks = [together & (gap < window) for window in (WINDOW, SEQ)]
    tables = []
    for base in rope_bases:
        cosine, sine = rotary_table(places, width, base)
        tables.append((cosine[:, None, :], sine[:, None, :]))

    current = moves.own_rows(layer_input)
    inputs, stores, weights, gains, qk_gains = [], [], [], [], []
    for level in range(2):
        w_query, w_keyval, extra = split_first(firsts[level], heads_width, width)
        weights.append((w_query, w_keyval) + split_second(seconds_low[level], heads_width, hidden_width))
        gain_rows, qk_gain = unpack_extra(extra, count_norms, width, dp)
        gains.append(gain_rows)
        qk_gains.append(qk_gain)
        inputs.append(current)
        norm_one = moves.spread(rms_scale(current, gain_rows[0]).astype(low))
        current, store = forward_layer(
            current, norm_one, weights[level], gain_rows, qk_gain, masks[level], tables[level], moves
        )
        stores.append(store)
    top = moves.my_rows(current)

    back = moves.own_rows(cotangent)
    shards = [None, None]
    for level in (1, 0):
        back_hidden, back_zone, wide, norm_grads = backward_ffn(
            weights[level], gains[level], stores[level], back, moves
        )
        back, grad_both, grad_outproj, grad_zero, grad_qk = backward_attention(
            inputs[level], weights[level], gains[level], qk_gains[level], stores[level],
            back_hidden, back_zone, masks[level], tables[level], moves,
        )
        gain_grads = jnp.stack((grad_zero,) + norm_grads) * moves.weight
        extra = pack_extra(gain_grads, grad_qk, dp)
        first_terms = jnp.concatenate([grad_both, extra], axis=1)
        second_terms = jnp.concatenate((grad_outproj,) + wide, axis=1)
        if level == 1:
            sums = scatter_native(jnp.concatenate([first_terms, second_terms], axis=1))
            first = sums[:, : first_terms.shape[1]]
            second = sums[:, first_terms.shape[1] :]
        else:
            second = scatter_native(second_terms)
            first = last_scatter(first_terms)
        shards[level] = (first, second)
    bottom = moves.my_rows(back)

    layers = []
    for first, second in shards:
        rows = first.shape[0]
        shared = moves.everywhere(first[:, heads_width:])
        grad_out, grad_gateup, grad_down = split_second(second, heads_width, hidden_width)
        extra = shared[:, 2 * width :]
        layers.append(
            (
                first[:, :heads_width],
                shared[:, : 2 * width],
                grad_out.T,
                jnp.stack([grad_gateup[:, :hidden_width], grad_gateup[:, hidden_width:]]),
                grad_down.T,
                extra[:, :count_norms].T,
                extra[: width // dp, count_norms : count_norms + 2].T,
            )
        )
    gradients = tuple(jnp.stack([a, b]) for a, b in zip(*layers))
    results = [adamw(*entry) for entry in zip(params, gradients, momenta, seconds)]
    return (
        (top, bottom)
        + gradients
        + tuple(entry[0] for entry in results)
        + tuple(entry[1] for entry in results)
        + tuple(entry[2] for entry in results)
    )


def solution(mesh):
    rows = P(("dp", "tensor"), None)
    weights = (
        P(None, "dp", "tensor"),
        P(None, "dp", None),
        P(None, "tensor", "dp"),
        P(None, None, "dp", "tensor"),
        P(None, "tensor", "dp"),
        P(None, None, "dp"),
        P(None, None, "dp"),
    )
    return jax.shard_map(
        on_device,
        mesh=mesh,
        in_specs=(rows, P("dp"), rows) + weights * 3,
        out_specs=(rows, rows) + weights * 4,
        check_vma=False,
    )
```

```python
import functools

import jax
import jax.numpy as jnp
from jax import lax
from jax.experimental import pallas as pl
from jax.experimental.pallas import tpu as pltpu
from jax.sharding import PartitionSpec as P

SEQ = 512
WINDOW = 256


norm_eps = 1e-06
rope_bases = (10000.0, 1000000.0)
learn_rate = 0.02
beta_first = 0.9
beta_second = 0.999
adam_eps = 1e-08
decay_rate = 0.1
adam_step = 4.0
masked_value = -1e30

low = jnp.bfloat16
full = jnp.float32

CORE_PAIRS = [(0, 1), (1, 0), (2, 3), (3, 2)]
CHIP_PAIRS = [(0, 2), (2, 0), (1, 3), (3, 1)]
CYCLE = (0, 2, 4, 6, 7, 5, 3, 1)
EXTRA = 128


def dot(left, right, dims):
    return lax.dot_general(left, right, (dims, ((), ())), preferred_element_type=full)


def rms_scale(values, gain):
    mean_sq = jnp.mean(values * values, axis=-1, keepdims=True)
    return values * lax.rsqrt(mean_sq + norm_eps) * (1.0 + gain)


def gated(gate, up):
    return jax.nn.gelu(gate, approximate=True) * up


def rotary_table(places, width, base):
    half = width // 2
    expo = jnp.arange(half, dtype=full) * (2.0 / width)
    freqs = jnp.exp(-expo * jnp.log(full(base)))
    angles = places.astype(full)[:, None] * freqs[None, :]
    return (jnp.cos(angles), jnp.sin(angles))


def tuned(mesh_sizes):
    return mesh_sizes == (8, 4)


def turn(step):
    count = len(CYCLE)
    return [(CYCLE[i], CYCLE[(i + step) % count]) for i in range(count)]


def at_cycle(position):
    place = position & 7
    return jnp.where(place < 4, 2 * place, 15 - 2 * place)


def my_place():
    me = lax.axis_index("dp")
    depth = me >> 1
    return jnp.where((me & 1) == 0, depth, 7 - depth)


def start_of(position, rows):
    return at_cycle(position) * rows


def put(out, piece, position, column=0):
    start = start_of(position, piece.shape[0])
    return lax.dynamic_update_slice(out, piece, (start, column))


def take(terms, position, column, columns):
    rows = terms.shape[0] // len(CYCLE)
    start = (start_of(position, rows), column)
    return lax.dynamic_slice(terms, start, (rows, columns)).astype(full)


class RingGather:
    def __init__(self, block):
        self.count = len(CYCLE)
        self.mine = my_place()
        self.step = 0
        out = jnp.zeros((self.count * block.shape[0], block.shape[1]), block.dtype)
        self.out = put(out, block, self.mine)
        self.ahead = self.behind = block

    def advance(self):
        self.step += 1
        self.ahead = lax.ppermute(self.ahead, "dp", turn(1))
        self.out = put(self.out, self.ahead, self.mine + self.count - self.step)
        if self.step < self.count // 2:
            self.behind = lax.ppermute(self.behind, "dp", turn(-1))
            self.out = put(self.out, self.behind, self.mine + self.step)

    def tie(self, value):
        self.ahead, self.behind, value = lax.optimization_barrier(
            (self.ahead, self.behind, value)
        )
        return value

    def finish(self):
        while self.step < self.count // 2:
            self.advance()
        return self.out


class NativeGather:
    def __init__(self, block):
        self.out = gather_native(block)

    def advance(self):
        pass

    def tie(self, value):
        return value

    def finish(self):
        return self.out


def whole_in_vmem(count):
    return [pl.BlockSpec(memory_space=pltpu.VMEM)] * count


def outer_kernel(widths, *refs):
    out = refs[-1]
    at = 0
    for i, width in enumerate(widths):
        terms = dot(refs[2 * i][...], refs[2 * i + 1][...], ((0,), (0,)))
        out[:, at : at + width] = terms.astype(low)
        at += width
    if at < out.shape[1]:
        out[:, at:] = refs[2 * len(widths)][...]


def outer_terms(pairs, extra=None):
    widths = tuple(right.shape[1] for _, right in pairs)
    operands = [entry for pair in pairs for entry in pair]
    total = sum(widths)
    if extra is not None:
        operands.append(extra)
        total += extra.shape[1]
    return pl.pallas_call(
        functools.partial(outer_kernel, widths),
        out_shape=jax.ShapeDtypeStruct((pairs[0][0].shape[1], total), low),
        in_specs=whole_in_vmem(len(operands)),
        out_specs=pl.BlockSpec(memory_space=pltpu.VMEM),
        name="outer_terms",
    )(*operands)


class HalfScatter:
    def __init__(self, terms):
        self.terms = terms
        self.columns = terms.shape[1]
        self.mine = my_place()
        self.half = len(CYCLE) // 2
        self.step = 0
        self.ahead = self.part(self.half)
        self.behind = self.part(self.half + 1)

    def part(self, steps):
        return take(self.terms, self.mine + steps, 0, self.columns)

    def done(self):
        return self.step == self.half

    def advance(self):
        self.step += 1
        self.ahead = lax.ppermute(self.ahead.astype(low), "dp", turn(1)).astype(full)
        if self.step < self.half:
            self.ahead = self.ahead + self.part(self.half - self.step)
            self.behind = lax.ppermute(self.behind.astype(low), "dp", turn(-1)).astype(full)
        if self.step < self.half - 1:
            self.behind = self.behind + self.part(self.half + 1 + self.step)

    def result(self):
        return self.ahead + self.behind + self.part(0)


def run_rings(rings, delays):
    count = 0
    while any(not ring.done() for ring in rings):
        active = [r for r, delay in zip(rings, delays) if count >= delay and not r.done()]
        for ring in active:
            ring.advance()
        moving = [ring for ring in active if not ring.done()]
        tied = lax.optimization_barrier(
            [(ring.ahead.astype(low), ring.behind.astype(low)) for ring in moving]
        )
        for ring, (ahead, behind) in zip(moving, tied):
            ring.ahead, ring.behind = ahead, behind
        count += 1
    return [ring.result() for ring in rings]


class WideScatter:
    def __init__(self, terms):
        self.terms = terms
        self.half = terms.shape[1] // 2
        self.mine = my_place()
        self.count = len(CYCLE)
        self.step = 0
        self.ahead = take(terms, self.mine + self.count - 1, 0, self.half)
        self.behind = take(terms, self.mine + 1, self.half, self.half)

    def tie(self, value):
        self.ahead, self.behind, value = lax.optimization_barrier(
            (self.ahead.astype(low), self.behind.astype(low), value)
        )
        return value

    def advance(self):
        self.step += 1
        ahead = lax.ppermute(self.ahead.astype(low), "dp", turn(1)).astype(full)
        behind = lax.ppermute(self.behind.astype(low), "dp", turn(-1)).astype(full)
        at = self.mine + 2 * self.count - 1 - self.step
        self.ahead = ahead + take(self.terms, at, 0, self.half)
        self.behind = behind + take(self.terms, self.mine + 1 + self.step, self.half, self.half)

    def done(self):
        return self.step == self.count - 1

    def result(self):
        return jnp.concatenate([self.ahead, self.behind], axis=1)


class NativeScatter:
    def __init__(self, terms):
        self.sums = scatter_native(terms)

    def tie(self, value):
        return value

    def advance(self):
        pass

    def done(self):
        return True

    def result(self):
        return self.sums


def gather_native(block):
    return lax.all_gather(block, "dp", axis=0, tiled=True)


def scatter_native(terms):
    return lax.psum_scatter(terms, "dp", scatter_dimension=0, tiled=True).astype(full)


class Pairs:
    def __init__(self, group):
        self.quarter = group // 4
        self.me = lax.axis_index("tensor")
        self.core = self.me % 2
        self.chip = self.me // 2
        self.group = group
        self.weight = 0.5

    def own_rows(self, values):
        other = lax.ppermute(values, "tensor", CHIP_PAIRS)
        first = jnp.where(self.chip == 0, values, other)
        second = jnp.where(self.chip == 0, other, values)
        return jnp.concatenate([first, second], axis=0)

    def my_rows(self, owned):
        return lax.dynamic_slice_in_dim(owned, self.chip * self.quarter, self.quarter, 0)

    def order(self):
        step = jnp.arange(self.quarter, dtype=jnp.int32)
        starts = (self.core, 2 + self.core, 1 - self.core, 3 - self.core)
        return jnp.concatenate([start * self.quarter + step for start in starts])

    def arrange(self, values):
        parts = [values[i * self.quarter : (i + 1) * self.quarter] for i in range(4)]
        swapped = jnp.concatenate([parts[1], parts[3], parts[0], parts[2]])
        return jnp.where(
            self.core == 0, jnp.concatenate([parts[0], parts[2], parts[1], parts[3]]), swapped
        )

    def spread(self, owned):
        return jnp.concatenate([owned, lax.ppermute(owned, "tensor", CORE_PAIRS)], axis=0)

    def split(self, partial):
        half = 2 * self.quarter
        return partial[:half], partial[half:].astype(low)

    def total(self, own, other):
        pair = own + lax.ppermute(other, "tensor", CORE_PAIRS).astype(full)
        return pair + lax.ppermute(pair.astype(low), "tensor", CHIP_PAIRS).astype(full)

    def everywhere(self, values, beside):
        pair = values + lax.ppermute(values.astype(low), "tensor", CORE_PAIRS).astype(full)
        other = lax.ppermute(pair.astype(low), "tensor", CHIP_PAIRS)
        other, beside = lax.optimization_barrier((other, beside))
        return pair + other.astype(full), beside


class Plain:
    def __init__(self, group):
        self.group = group
        self.weight = 1.0

    def own_rows(self, values):
        return values

    def my_rows(self, owned):
        return owned

    def order(self):
        return jnp.arange(self.group, dtype=jnp.int32)

    def arrange(self, values):
        return values

    def spread(self, owned):
        return lax.all_gather(owned, "tensor", axis=0, tiled=True)

    def split(self, partial):
        half = self.group // 2
        return partial[:half], partial[half:].astype(low)

    def total(self, own, other):
        partial = jnp.concatenate([own.astype(low), other])
        return lax.psum_scatter(partial, "tensor", scatter_dimension=0, tiled=True).astype(full)

    def everywhere(self, values, beside):
        return lax.psum(values.astype(low), "tensor").astype(full), beside


def pad_rows(values, rows):
    return jnp.pad(values, ((0, rows - values.shape[0]), (0, 0)))


def pack_layer(params, level):
    query, keyval, outproj, gateup, down, gains, qk_gains = (
        param[level].astype(low) for param in params
    )
    rows = query.shape[0]
    extra = jnp.concatenate([gains.T, pad_rows(qk_gains.T, rows)], axis=1)
    extra = jnp.pad(extra, ((0, 0), (0, EXTRA - extra.shape[1])))
    first = jnp.concatenate([query, keyval, extra], axis=1)
    return first, outproj.T, jnp.concatenate([gateup[0], gateup[1], down.T], axis=1)


def unpack_extra(extra, count_norms, width, dp):
    gains = extra[:, :count_norms].astype(full).T
    rows = extra.shape[0] // dp
    qk = extra[:, count_norms : count_norms + 2].reshape(dp, rows, 2)[:, : width // dp]
    return gains, qk.reshape(width, 2).astype(full).T


def pack_extra(gains, qk, dp):
    width = qk.shape[1]
    rows = gains.shape[1] // dp
    spread = jnp.pad(qk.T.reshape(dp, width // dp, 2), ((0, 0), (0, rows - width // dp), (0, 0)))
    return jnp.concatenate([gains.T, spread.reshape(dp * rows, 2)], axis=1).astype(low)


def turned(values, cosine, sine):
    half = values.shape[1] // 2
    first, second = values[:, :half], values[:, half:]
    return first * cosine - second * sine, second * cosine + first * sine


def turned_back(values, cosine, sine):
    half = values.shape[1] // 2
    first, second = values[:, :half], values[:, half:]
    back = (first * cosine + second * sine, second * cosine - first * sine)
    return jnp.concatenate(back, axis=1)


def inverse_rms(values):
    return lax.rsqrt(jnp.mean(values * values, axis=1, keepdims=True) + norm_eps)


def allowed_pairs(column, row, window):
    gap = column[:, 0:1] - row[0:1, :]
    return (gap >= 0) & (gap < window) & (column[:, 1:2] == row[1:2, :])


def attend_kernel(
    window, norm_ref, w_ref, gain_ref, cos_ref, sin_ref, column_ref, row_ref,
    q_ref, k_ref, v_ref, mixed_ref, logsum_ref, qraw_ref, kraw_ref,
):
    group = norm_ref.shape[0]
    width = gain_ref.shape[1]
    half = width // 2
    wide = min(group, 256)

    def project(step, carry):
        rows = pl.ds(pl.multiple_of(step * wide, wide), wide)
        raw = dot(norm_ref[rows, :], w_ref[:, : 3 * width], ((1,), (0,)))
        for at, (raw_ref, low_ref) in enumerate(((qraw_ref, q_ref), (kraw_ref, k_ref))):
            value = raw[:, at * width : (at + 1) * width]
            raw_ref[rows, :] = value
            scaled = value * inverse_rms(value) * (1.0 + gain_ref[at : at + 1, :])
            first, second = turned(scaled, cos_ref[rows, :], sin_ref[rows, :])
            low_ref[rows, :half] = first.astype(low)
            low_ref[rows, half:] = second.astype(low)
        v_ref[rows, :] = raw[:, 2 * width : 3 * width].astype(low)
        return carry

    lax.fori_loop(0, group // wide, project, 0)
    narrow = min(group, 128)

    def attend(step, carry):
        rows = pl.ds(pl.multiple_of(step * narrow, narrow), narrow)
        scores = dot(q_ref[rows, :], k_ref[...], ((1,), (1,))) * (width**-0.5)
        allowed = allowed_pairs(column_ref[rows, :], row_ref[...], window)
        scores = jnp.where(allowed, scores, masked_value)
        peak = jnp.max(scores, axis=1, keepdims=True)
        powers = jnp.exp(scores - peak)
        total = jnp.sum(powers, axis=1, keepdims=True)
        logsum_ref[rows, :] = peak + jnp.log(total)
        probs = (powers * (1.0 / total)).astype(low)
        mixed_ref[rows, :] = dot(probs, v_ref[...], ((1,), (0,))).astype(low)
        return carry

    lax.fori_loop(0, group // narrow, attend, 0)


def attend_back_kernel(
    window, zone_ref, wout_ref, w_ref, q_ref, k_ref, v_ref, logsum_ref, qraw_ref, kraw_ref,
    gain_ref, cos_ref, sin_ref, column_ref, row_ref,
    both_ref, own_ref, other_ref, gain_back_ref, dk_ref, dv_ref,
):
    group = zone_ref.shape[0]
    width = gain_ref.shape[1]
    scale = width**-0.5
    narrow = min(group, 128)
    dk_ref[...] = jnp.zeros_like(dk_ref)
    dv_ref[...] = jnp.zeros_like(dv_ref)

    def undo(at, back, raw, rows):
        back = turned_back(back, cos_ref[rows, :], sin_ref[rows, :])
        inverse = inverse_rms(raw)
        shape = raw * inverse
        scaled = back * (1.0 + gain_ref[at : at + 1, :])
        mean = jnp.mean(scaled * shape, axis=1, keepdims=True)
        result = inverse * (scaled - shape * mean)
        both_ref[rows, at * width : (at + 1) * width] = result.astype(low)
        return jnp.sum(back * shape, axis=0, keepdims=True)

    def queries(step, carry):
        rows = pl.ds(pl.multiple_of(step * narrow, narrow), narrow)
        back_mixed = dot(zone_ref[rows, :], wout_ref[...], ((1,), (0,))).astype(low)
        scores = dot(q_ref[rows, :], k_ref[...], ((1,), (1,))) * scale
        allowed = allowed_pairs(column_ref[rows, :], row_ref[...], window)
        probs = jnp.exp(jnp.where(allowed, scores, masked_value) - logsum_ref[rows, :])
        back_probs = dot(back_mixed, v_ref[...], ((1,), (1,)))
        delta = jnp.sum(probs * back_probs, axis=1, keepdims=True)
        back_scores = (probs * (back_probs - delta) * scale).astype(low)
        dk_ref[...] += dot(back_scores, q_ref[rows, :], ((0,), (0,)))
        dv_ref[...] += dot(probs.astype(low), back_mixed, ((0,), (0,)))
        back_query = dot(back_scores, k_ref[...], ((1,), (0,)))
        return carry + undo(0, back_query, qraw_ref[rows, :], rows)

    def keys(step, carry):
        rows = pl.ds(pl.multiple_of(step * narrow, narrow), narrow)
        both_ref[rows, 2 * width :] = dv_ref[rows, :].astype(low)
        return carry + undo(1, dk_ref[rows, :], kraw_ref[rows, :], rows)

    zero = jnp.zeros((1, width), full)
    gain_back_ref[0:1, :] = lax.fori_loop(0, group // narrow, queries, zero)
    gain_back_ref[1:2, :] = lax.fori_loop(0, group // narrow, keys, zero)
    half = group // 2
    w_all = w_ref[:, : 3 * width]
    own_ref[...] = dot(both_ref[:half, :], w_all, ((1,), (1,)))
    other_ref[...] = dot(both_ref[half:, :], w_all, ((1,), (1,))).astype(low)


def columns_of(array, at, columns):
    block = at // columns
    if array.shape[1] == columns:
        return array, pl.BlockSpec(array.shape, lambda i: (0, 0))
    if at % columns:
        array = array[:, at : at + columns]
        block = 0
    return array, pl.BlockSpec((array.shape[0], columns), lambda i: (0, block))


def run_kernel(kernel, name, operands, outs, scratch=()):
    arrays, specs = [], []
    for entry in operands:
        array, spec = entry if isinstance(entry, tuple) else columns_of(entry, 0, entry.shape[1])
        arrays.append(array)
        specs.append(spec)
    return pl.pallas_call(
        kernel,
        grid=(1,),
        out_shape=[jax.ShapeDtypeStruct(shape, kind) for shape, kind in outs],
        in_specs=specs,
        out_specs=[pl.BlockSpec(shape, lambda i: (0, 0)) for shape, _ in outs],
        scratch_shapes=scratch,
        name=name,
    )(*arrays)


def forward_attention(norm_one, w_first, qk_gain, window, table, places):
    group, width = norm_one.shape[0], qk_gain.shape[1]
    square = (group, width)
    return run_kernel(
        functools.partial(attend_kernel, window),
        "attend",
        (norm_one, w_first, qk_gain, *table, *places),
        [(square, low)] * 4 + [((group, 1), full)] + [(square, full)] * 2,
    )


def forward_rest(x_own, attn_flat, weights, gain_rows, moves):
    w_outproj, w_gateup, w_down = weights
    z_one = moves.total(*moves.split(dot(attn_flat, w_outproj, ((1,), (1,)))))
    hidden = x_own + rms_scale(z_one, gain_rows[1])
    norm_three = moves.spread(rms_scale(hidden, gain_rows[2]).astype(low))
    both = dot(norm_three, w_gateup, ((1,), (0,)))
    half = both.shape[1] // 2
    act = gated(both[:, :half], both[:, half:]).astype(low)
    z_two = moves.total(*moves.split(dot(act, w_down, ((1,), (1,)))))
    result = hidden + rms_scale(z_two, gain_rows[3])
    return result, (z_one, hidden, norm_three, both, act, z_two)


def backward_ffn(weights, gain_rows, saved, back_out, moves):
    z_one, hidden, norm_three, both, act, z_two = saved
    w_outproj, w_gateup, w_down = weights
    half = both.shape[1] // 2
    back_ztwo, grad_three = jax.vjp(rms_scale, z_two, gain_rows[3])[1](back_out)
    ztwo_low = moves.spread(back_ztwo.astype(low))
    back_act = dot(ztwo_low, w_down, ((1,), (0,)))
    back_gate, back_up = jax.vjp(gated, both[:, :half], both[:, half:])[1](back_act)
    both_low = jnp.concatenate([back_gate.astype(low), back_up.astype(low)], axis=1)
    back_three = moves.total(*moves.split(dot(both_low, w_gateup, ((1,), (1,)))))
    back_hnorm, grad_two = jax.vjp(rms_scale, hidden, gain_rows[2])[1](back_three)
    back_hidden = back_out + back_hnorm
    back_zone, grad_one = jax.vjp(rms_scale, z_one, gain_rows[1])[1](back_hidden)
    wide = [(norm_three, both_low), (ztwo_low, act)]
    return back_hidden, back_zone, wide, (grad_one, grad_two, grad_three)


def backward_attention(x_own, norm_one, w_first, w_out, gain_rows, qk_gain, attended, back_hidden, zone_low, window, table, places, moves, beside):
    q_low, k_low, v_low, mixed, logsum, qraw, kraw = attended
    group, width = qraw.shape
    model = norm_one.shape[1]
    both, own, other, grad_qk = run_kernel(
        functools.partial(attend_back_kernel, window),
        "attend_back",
        (zone_low, w_out, w_first, q_low, k_low, v_low, logsum, qraw, kraw, qk_gain, *table, *places),
        [
            ((group, 3 * width), low),
            ((group // 2, model), full),
            ((group // 2, model), low),
            ((2, width), full),
        ],
        [pltpu.VMEM((group, width), full)] * 2,
    )
    if beside is not None:
        own = beside.tie(own)
        beside.advance()
    back_one = moves.total(own, other)
    if beside is not None:
        back_one = beside.tie(back_one)
    back_xnorm, grad_zero = jax.vjp(rms_scale, x_own, gain_rows[0])[1](back_one)
    return back_hidden + back_xnorm, (norm_one, both), grad_zero, grad_qk


def adamw(param, grad, moment, second):
    moment_new = beta_first * moment + (1.0 - beta_first) * grad
    second_new = beta_second * second + (1.0 - beta_second) * grad * grad
    moment_hat = moment_new / (1.0 - beta_first**adam_step)
    second_hat = second_new / (1.0 - beta_second**adam_step)
    updated = param - learn_rate * (
        moment_hat / (jnp.sqrt(second_hat) + adam_eps) + decay_rate * param
    )
    return (updated, moment_new, second_new)


def on_device(layer_input, positions, cotangent, *state):
    params, momenta, seconds = state[:7], state[7:14], state[14:]
    dp = lax.axis_size("dp")
    fast = tuned((dp, lax.axis_size("tensor")))
    group = positions.shape[0]
    heads_width = params[0].shape[2]
    hidden_width = params[3].shape[3]
    count_norms = params[5].shape[1]
    width = params[6].shape[2] * dp
    moves = Pairs(group) if fast else Plain(group)
    first_gather = RingGather if fast else NativeGather
    wide_scatter = WideScatter if fast else NativeScatter
    half_scatter = HalfScatter if fast else NativeScatter

    packs = [pack_layer(params, level) for level in range(2)]
    firsts = [first_gather(packs[0][0]).finish()]
    wides = [gather_native(jnp.concatenate(packs[0][1:], axis=1)), gather_native(packs[1][2])]
    first_columns = packs[0][0].shape[1]

    where_at = moves.order()
    places = moves.arrange(positions)
    marks = (where_at, places - where_at)
    marks = (jnp.stack(marks, axis=1), jnp.stack(marks, axis=0))
    windows = (WINDOW, SEQ)
    tables = [rotary_table(places, width, base) for base in rope_bases]

    current = moves.own_rows(layer_input)
    inputs, norms, attends, stores, gains, qk_gains, outs, rests = ([] for _ in range(8))
    for level in range(2):
        extra = firsts[level][:, 3 * width : first_columns]
        gain_rows, qk_gain = unpack_extra(extra, count_norms, width, dp)
        gains.append(gain_rows)
        qk_gains.append(qk_gain)
        inputs.append(current)
        norm_one = moves.spread(rms_scale(current, gain_rows[0]).astype(low))
        norms.append(norm_one)
        attended = forward_attention(
            norm_one, firsts[level], qk_gain, windows[level], tables[level], marks
        )
        if level == 0:
            block = jnp.concatenate(packs[1][:2], axis=1)
            block, mixed = lax.optimization_barrier((block, attended[3]))
            attended = (*attended[:3], mixed, *attended[4:])
            ring = first_gather(block)
            ring.advance()
            ring.advance()
            w_wide = ring.tie(wides[0])
            firsts.append(ring.finish())
            outs.append((w_wide[:, :heads_width], columns_of(w_wide, 0, heads_width)))
            w_wide = w_wide[:, heads_width:]
        else:
            w_out = firsts[1][:, first_columns:]
            outs.append((w_out, columns_of(w_out, 0, heads_width)))
            w_wide = wides[1]
        rests.append((outs[level][0], w_wide[:, : 2 * hidden_width], w_wide[:, 2 * hidden_width :]))
        attends.append(attended)
        current, store = forward_rest(current, attended[3], rests[level], gain_rows, moves)
        stores.append(store)
    top = moves.my_rows(current)

    back = moves.own_rows(cotangent)
    shards = [None, None]
    extra_grads = []
    for level in (1, 0):
        back_hidden, back_zone, wide, norm_grads = backward_ffn(
            rests[level], gains[level], stores[level], back, moves
        )
        zone_low = moves.spread(back_zone.astype(low))
        beside = None
        if level == 0:
            beside = wide_scatter(outer_terms(wide))
            zone_low = beside.tie(zone_low)
            beside.advance()
        outer = (zone_low, attends[level][3])
        back, narrow, grad_zero, grad_qk = backward_attention(
            inputs[level], norms[level], firsts[level], outs[level][1], gains[level],
            qk_gains[level], attends[level], back_hidden, zone_low, windows[level],
            tables[level], marks, moves, beside,
        )
        gain_grads = jnp.stack((grad_zero,) + norm_grads) * moves.weight
        extra_grads.append(pack_extra(gain_grads, grad_qk, dp))
        if level == 1:
            terms = outer_terms([narrow, outer] + wide)
            terms, back = lax.optimization_barrier((terms, back))
            sums = scatter_native(terms)
            columns = 3 * width + heads_width
            shards[1] = (sums[:, :columns], sums[:, columns:])
        else:
            slim = half_scatter(outer_terms([narrow, outer]))
    extra_columns = extra_grads[0].shape[1]
    extra = jnp.concatenate(extra_grads[::-1], axis=1)
    extra = half_scatter(jnp.pad(extra, ((0, 0), (0, EXTRA - 2 * extra_columns))))
    first, second, extra = run_rings([slim, beside, extra], [0, 0, 2])
    shards[0] = (first, second)
    bottom = moves.my_rows(back)

    keyvals = [first[:, heads_width : 3 * width] for first, _ in shards]
    early, _ = moves.everywhere(keyvals[1], ())
    big = [
        jnp.stack([first[:, :heads_width] for first, _ in shards]),
        jnp.stack([first[:, 3 * width :].T for first, _ in shards]),
        jnp.stack(
            [
                jnp.stack([second[:, :hidden_width], second[:, hidden_width : 2 * hidden_width]])
                for _, second in shards
            ]
        ),
        jnp.stack([second[:, 2 * hidden_width :].T for _, second in shards]),
    ]
    big_results = [
        adamw(params[at], grad, momenta[at], seconds[at]) for at, grad in zip((0, 2, 3, 4), big)
    ]
    last = jnp.concatenate([keyvals[0], extra], axis=1)
    shared, big_results = moves.everywhere(last, big_results)
    extras = [
        shared[:, 2 * width + level * extra_columns :][:, :extra_columns] for level in range(2)
    ]
    small = [
        jnp.stack([shared[:, : 2 * width], early]),
        jnp.stack([extra[:, :count_norms].T for extra in extras]),
        jnp.stack([extra[: width // dp, count_norms:].T for extra in extras]),
    ]
    small_results = [
        adamw(params[at], grad, momenta[at], seconds[at]) for at, grad in zip((1, 5, 6), small)
    ]
    gradients = (big[0], small[0], big[1], big[2], big[3], small[1], small[2])
    results = [
        big_results[0], small_results[0], *big_results[1:], small_results[1], small_results[2],
    ]
    return (
        (top, bottom)
        + gradients
        + tuple(entry[0] for entry in results)
        + tuple(entry[1] for entry in results)
        + tuple(entry[2] for entry in results)
    )


def solution(mesh):
    rows = P(("dp", "tensor"), None)
    weights = (
        P(None, "dp", "tensor"),
        P(None, "dp", None),
        P(None, "tensor", "dp"),
        P(None, None, "dp", "tensor"),
        P(None, "tensor", "dp"),
        P(None, None, "dp"),
        P(None, None, "dp"),
    )
    return jax.shard_map(
        on_device,
        mesh=mesh,
        in_specs=(rows, P("dp"), rows) + weights * 3,
        out_specs=(rows, rows) + weights * 4,
        check_vma=False,
    )
```

```python
import functools

import jax
import jax.numpy as jnp
from jax import lax
from jax.experimental import pallas as pl
from jax.experimental.pallas import tpu as pltpu
from jax.sharding import PartitionSpec as P

SEQ = 512
WINDOW = 256


norm_eps = 1e-06
rope_bases = (10000.0, 1000000.0)
learn_rate = 0.02
beta_first = 0.9
beta_second = 0.999
adam_eps = 1e-08
decay_rate = 0.1
adam_step = 4.0
masked_value = -1e30

low = jnp.bfloat16
full = jnp.float32

CORE_PAIRS = [(0, 1), (1, 0), (2, 3), (3, 2)]
CHIP_PAIRS = [(0, 2), (2, 0), (1, 3), (3, 1)]
CYCLE = (0, 2, 4, 6, 7, 5, 3, 1)
EXTRA = 128


def dot(left, right, dims):
    return lax.dot_general(left, right, (dims, ((), ())), preferred_element_type=full)


def rms_scale(values, gain):
    mean_sq = jnp.mean(values * values, axis=-1, keepdims=True)
    return values * lax.rsqrt(mean_sq + norm_eps) * (1.0 + gain)


def gated(gate, up):
    return jax.nn.gelu(gate, approximate=True) * up


def rotary_table(places, width, base):
    half = width // 2
    expo = jnp.arange(half, dtype=full) * (2.0 / width)
    freqs = jnp.exp(-expo * jnp.log(full(base)))
    angles = places.astype(full)[:, None] * freqs[None, :]
    return (jnp.cos(angles), jnp.sin(angles))


def tuned(mesh_sizes):
    return mesh_sizes == (8, 4)


def turn(step):
    count = len(CYCLE)
    return [(CYCLE[i], CYCLE[(i + step) % count]) for i in range(count)]


def at_cycle(position):
    place = position & 7
    return jnp.where(place < 4, 2 * place, 15 - 2 * place)


def my_place():
    me = lax.axis_index("dp")
    depth = me >> 1
    return jnp.where((me & 1) == 0, depth, 7 - depth)


def start_of(position, rows):
    return at_cycle(position) * rows


def put(out, piece, position, column=0):
    start = start_of(position, piece.shape[0])
    return lax.dynamic_update_slice(out, piece, (start, column))


def take(terms, position, column, columns):
    rows = terms.shape[0] // len(CYCLE)
    start = (start_of(position, rows), column)
    return lax.dynamic_slice(terms, start, (rows, columns)).astype(full)


class RingGather:
    def __init__(self, block):
        self.count = len(CYCLE)
        self.mine = my_place()
        self.step = 0
        out = jnp.zeros((self.count * block.shape[0], block.shape[1]), block.dtype)
        self.out = put(out, block, self.mine)
        self.ahead = self.behind = block

    def advance(self):
        self.step += 1
        self.ahead = lax.ppermute(self.ahead, "dp", turn(1))
        self.out = put(self.out, self.ahead, self.mine + self.count - self.step)
        if self.step < self.count // 2:
            self.behind = lax.ppermute(self.behind, "dp", turn(-1))
            self.out = put(self.out, self.behind, self.mine + self.step)

    def tie(self, value):
        self.ahead, self.behind, value = lax.optimization_barrier(
            (self.ahead, self.behind, value)
        )
        return value

    def finish(self):
        while self.step < self.count // 2:
            self.advance()
        return self.out


class NativeGather:
    def __init__(self, block):
        self.out = gather_native(block)

    def advance(self):
        pass

    def tie(self, value):
        return value

    def finish(self):
        return self.out


def whole_in_vmem(count):
    return [pl.BlockSpec(memory_space=pltpu.VMEM)] * count


def outer_kernel(widths, *refs):
    out = refs[-1]
    at = 0
    for i, width in enumerate(widths):
        terms = dot(refs[2 * i][...], refs[2 * i + 1][...], ((0,), (0,)))
        out[:, at : at + width] = terms.astype(low)
        at += width
    if at < out.shape[1]:
        out[:, at:] = refs[2 * len(widths)][...]


def outer_terms(pairs, extra=None):
    widths = tuple(right.shape[1] for _, right in pairs)
    operands = [entry for pair in pairs for entry in pair]
    total = sum(widths)
    if extra is not None:
        operands.append(extra)
        total += extra.shape[1]
    return pl.pallas_call(
        functools.partial(outer_kernel, widths),
        out_shape=jax.ShapeDtypeStruct((pairs[0][0].shape[1], total), low),
        in_specs=whole_in_vmem(len(operands)),
        out_specs=pl.BlockSpec(memory_space=pltpu.VMEM),
        name="outer_terms",
    )(*operands)


class HalfScatter:
    def __init__(self, terms):
        self.terms = terms
        self.columns = terms.shape[1]
        self.mine = my_place()
        self.half = len(CYCLE) // 2
        self.step = 0
        self.ahead = self.part(self.half)
        self.behind = self.part(self.half + 1)

    def part(self, steps):
        return take(self.terms, self.mine + steps, 0, self.columns)

    def done(self):
        return self.step == self.half

    def advance(self):
        self.step += 1
        self.ahead = lax.ppermute(self.ahead.astype(low), "dp", turn(1)).astype(full)
        if self.step < self.half:
            self.ahead = self.ahead + self.part(self.half - self.step)
            self.behind = lax.ppermute(self.behind.astype(low), "dp", turn(-1)).astype(full)
        if self.step < self.half - 1:
            self.behind = self.behind + self.part(self.half + 1 + self.step)

    def result(self):
        return self.ahead + self.behind + self.part(0)


def run_rings(rings, delays):
    count = 0
    while any(not ring.done() for ring in rings):
        active = [r for r, delay in zip(rings, delays) if count >= delay and not r.done()]
        for ring in active:
            ring.advance()
        moving = [ring for ring in active if not ring.done()]
        tied = lax.optimization_barrier(
            [(ring.ahead.astype(low), ring.behind.astype(low)) for ring in moving]
        )
        for ring, (ahead, behind) in zip(moving, tied):
            ring.ahead, ring.behind = ahead, behind
        count += 1
    return [ring.result() for ring in rings]


class WideScatter:
    def __init__(self, terms):
        self.terms = terms
        self.half = terms.shape[1] // 2
        self.mine = my_place()
        self.count = len(CYCLE)
        self.step = 0
        self.ahead = take(terms, self.mine + self.count - 1, 0, self.half)
        self.behind = take(terms, self.mine + 1, self.half, self.half)

    def tie(self, value):
        self.ahead, self.behind, value = lax.optimization_barrier(
            (self.ahead.astype(low), self.behind.astype(low), value)
        )
        return value

    def advance(self):
        self.step += 1
        ahead = lax.ppermute(self.ahead.astype(low), "dp", turn(1)).astype(full)
        behind = lax.ppermute(self.behind.astype(low), "dp", turn(-1)).astype(full)
        at = self.mine + 2 * self.count - 1 - self.step
        self.ahead = ahead + take(self.terms, at, 0, self.half)
        self.behind = behind + take(self.terms, self.mine + 1 + self.step, self.half, self.half)

    def done(self):
        return self.step == self.count - 1

    def result(self):
        return jnp.concatenate([self.ahead, self.behind], axis=1)


class NativeScatter:
    def __init__(self, terms):
        self.sums = scatter_native(terms)

    def tie(self, value):
        return value

    def advance(self):
        pass

    def done(self):
        return True

    def result(self):
        return self.sums


def gather_native(block):
    return lax.all_gather(block, "dp", axis=0, tiled=True)


def scatter_native(terms):
    return lax.psum_scatter(terms, "dp", scatter_dimension=0, tiled=True).astype(full)


class Pairs:
    def __init__(self, group):
        self.quarter = group // 4
        self.me = lax.axis_index("tensor")
        self.core = self.me % 2
        self.chip = self.me // 2
        self.group = group
        self.weight = 0.5

    def own_rows(self, values):
        other = lax.ppermute(values, "tensor", CHIP_PAIRS)
        first = jnp.where(self.chip == 0, values, other)
        second = jnp.where(self.chip == 0, other, values)
        return jnp.concatenate([first, second], axis=0)

    def my_rows(self, owned):
        return lax.dynamic_slice_in_dim(owned, self.chip * self.quarter, self.quarter, 0)

    def order(self):
        step = jnp.arange(self.quarter, dtype=jnp.int32)
        starts = (self.core, 2 + self.core, 1 - self.core, 3 - self.core)
        return jnp.concatenate([start * self.quarter + step for start in starts])

    def arrange(self, values):
        parts = [values[i * self.quarter : (i + 1) * self.quarter] for i in range(4)]
        swapped = jnp.concatenate([parts[1], parts[3], parts[0], parts[2]])
        return jnp.where(
            self.core == 0, jnp.concatenate([parts[0], parts[2], parts[1], parts[3]]), swapped
        )

    def spread(self, owned):
        return jnp.concatenate([owned, lax.ppermute(owned, "tensor", CORE_PAIRS)], axis=0)

    def split(self, partial):
        half = 2 * self.quarter
        return partial[:half], partial[half:].astype(low)

    def total(self, own, other):
        pair = own + lax.ppermute(other, "tensor", CORE_PAIRS).astype(full)
        return pair + lax.ppermute(pair.astype(low), "tensor", CHIP_PAIRS).astype(full)

    def everywhere(self, values, beside):
        pair = values + lax.ppermute(values.astype(low), "tensor", CORE_PAIRS).astype(full)
        other = lax.ppermute(pair.astype(low), "tensor", CHIP_PAIRS)
        other, beside = lax.optimization_barrier((other, beside))
        return pair + other.astype(full), beside


class Plain:
    def __init__(self, group):
        self.group = group
        self.weight = 1.0

    def own_rows(self, values):
        return values

    def my_rows(self, owned):
        return owned

    def order(self):
        return jnp.arange(self.group, dtype=jnp.int32)

    def arrange(self, values):
        return values

    def spread(self, owned):
        return lax.all_gather(owned, "tensor", axis=0, tiled=True)

    def split(self, partial):
        half = self.group // 2
        return partial[:half], partial[half:].astype(low)

    def total(self, own, other):
        partial = jnp.concatenate([own.astype(low), other])
        return lax.psum_scatter(partial, "tensor", scatter_dimension=0, tiled=True).astype(full)

    def everywhere(self, values, beside):
        return lax.psum(values.astype(low), "tensor").astype(full), beside


def pad_rows(values, rows):
    return jnp.pad(values, ((0, rows - values.shape[0]), (0, 0)))


def pack_layer(params, level):
    query, keyval, outproj, gateup, down, gains, qk_gains = (
        param[level].astype(low) for param in params
    )
    rows = query.shape[0]
    extra = jnp.concatenate([gains.T, pad_rows(qk_gains.T, rows)], axis=1)
    extra = jnp.pad(extra, ((0, 0), (0, EXTRA - extra.shape[1])))
    first = jnp.concatenate([query, keyval, extra], axis=1)
    return first, outproj.T, jnp.concatenate([gateup[0], gateup[1], down.T], axis=1)


def unpack_extra(extra, count_norms, width, dp):
    gains = extra[:, :count_norms].astype(full).T
    rows = extra.shape[0] // dp
    qk = extra[:, count_norms : count_norms + 2].reshape(dp, rows, 2)[:, : width // dp]
    return gains, qk.reshape(width, 2).astype(full).T


def pack_extra(gains, qk, dp):
    width = qk.shape[1]
    rows = gains.shape[1] // dp
    spread = jnp.pad(qk.T.reshape(dp, width // dp, 2), ((0, 0), (0, rows - width // dp), (0, 0)))
    return jnp.concatenate([gains.T, spread.reshape(dp * rows, 2)], axis=1).astype(low)


def turned(values, cosine, sine):
    half = values.shape[1] // 2
    first, second = values[:, :half], values[:, half:]
    return first * cosine - second * sine, second * cosine + first * sine


def turned_back(values, cosine, sine):
    half = values.shape[1] // 2
    first, second = values[:, :half], values[:, half:]
    back = (first * cosine + second * sine, second * cosine - first * sine)
    return jnp.concatenate(back, axis=1)


def inverse_rms(values):
    return lax.rsqrt(jnp.mean(values * values, axis=1, keepdims=True) + norm_eps)


def allowed_pairs(column, row, window):
    gap = column[:, 0:1] - row[0:1, :]
    return (gap >= 0) & (gap < window) & (column[:, 1:2] == row[1:2, :])


def attend_kernel(
    window, norm_ref, w_ref, gain_ref, cos_ref, sin_ref, column_ref, row_ref,
    q_ref, k_ref, v_ref, mixed_ref, logsum_ref, qraw_ref, kraw_ref,
):
    group = norm_ref.shape[0]
    width = gain_ref.shape[1]
    half = width // 2
    wide = min(group, 256)

    def project(step, carry):
        rows = pl.ds(pl.multiple_of(step * wide, wide), wide)
        raw = dot(norm_ref[rows, :], w_ref[:, : 3 * width], ((1,), (0,)))
        for at, (raw_ref, low_ref) in enumerate(((qraw_ref, q_ref), (kraw_ref, k_ref))):
            value = raw[:, at * width : (at + 1) * width]
            raw_ref[rows, :] = value
            scaled = value * inverse_rms(value) * (1.0 + gain_ref[at : at + 1, :])
            first, second = turned(scaled, cos_ref[rows, :], sin_ref[rows, :])
            low_ref[rows, :half] = first.astype(low)
            low_ref[rows, half:] = second.astype(low)
        v_ref[rows, :] = raw[:, 2 * width : 3 * width].astype(low)
        return carry

    lax.fori_loop(0, group // wide, project, 0)
    narrow = min(group, 128)

    def attend(step, carry):
        rows = pl.ds(pl.multiple_of(step * narrow, narrow), narrow)
        scores = dot(q_ref[rows, :], k_ref[...], ((1,), (1,))) * (width**-0.5)
        allowed = allowed_pairs(column_ref[rows, :], row_ref[...], window)
        scores = jnp.where(allowed, scores, masked_value)
        peak = jnp.max(scores, axis=1, keepdims=True)
        powers = jnp.exp(scores - peak)
        total = jnp.sum(powers, axis=1, keepdims=True)
        logsum_ref[rows, :] = peak + jnp.log(total)
        probs = (powers * (1.0 / total)).astype(low)
        mixed_ref[rows, :] = dot(probs, v_ref[...], ((1,), (0,))).astype(low)
        return carry

    lax.fori_loop(0, group // narrow, attend, 0)


def attend_back_kernel(
    window, zone_ref, wout_ref, w_ref, q_ref, k_ref, v_ref, logsum_ref, qraw_ref, kraw_ref,
    gain_ref, cos_ref, sin_ref, column_ref, row_ref,
    both_ref, own_ref, other_ref, gain_back_ref, dk_ref, dv_ref,
):
    group = zone_ref.shape[0]
    width = gain_ref.shape[1]
    scale = width**-0.5
    narrow = min(group, 128)
    dk_ref[...] = jnp.zeros_like(dk_ref)
    dv_ref[...] = jnp.zeros_like(dv_ref)

    def undo(at, back, raw, rows):
        back = turned_back(back, cos_ref[rows, :], sin_ref[rows, :])
        inverse = inverse_rms(raw)
        shape = raw * inverse
        scaled = back * (1.0 + gain_ref[at : at + 1, :])
        mean = jnp.mean(scaled * shape, axis=1, keepdims=True)
        result = inverse * (scaled - shape * mean)
        both_ref[rows, at * width : (at + 1) * width] = result.astype(low)
        return jnp.sum(back * shape, axis=0, keepdims=True)

    def queries(step, carry):
        rows = pl.ds(pl.multiple_of(step * narrow, narrow), narrow)
        back_mixed = dot(zone_ref[rows, :], wout_ref[...], ((1,), (0,))).astype(low)
        scores = dot(q_ref[rows, :], k_ref[...], ((1,), (1,))) * scale
        allowed = allowed_pairs(column_ref[rows, :], row_ref[...], window)
        probs = jnp.exp(jnp.where(allowed, scores, masked_value) - logsum_ref[rows, :])
        back_probs = dot(back_mixed, v_ref[...], ((1,), (1,)))
        delta = jnp.sum(probs * back_probs, axis=1, keepdims=True)
        back_scores = (probs * (back_probs - delta) * scale).astype(low)
        dk_ref[...] += dot(back_scores, q_ref[rows, :], ((0,), (0,)))
        dv_ref[...] += dot(probs.astype(low), back_mixed, ((0,), (0,)))
        back_query = dot(back_scores, k_ref[...], ((1,), (0,)))
        return carry + undo(0, back_query, qraw_ref[rows, :], rows)

    def keys(step, carry):
        rows = pl.ds(pl.multiple_of(step * narrow, narrow), narrow)
        both_ref[rows, 2 * width :] = dv_ref[rows, :].astype(low)
        return carry + undo(1, dk_ref[rows, :], kraw_ref[rows, :], rows)

    zero = jnp.zeros((1, width), full)
    gain_back_ref[0:1, :] = lax.fori_loop(0, group // narrow, queries, zero)
    gain_back_ref[1:2, :] = lax.fori_loop(0, group // narrow, keys, zero)
    half = group // 2
    w_all = w_ref[:, : 3 * width]
    own_ref[...] = dot(both_ref[:half, :], w_all, ((1,), (1,)))
    other_ref[...] = dot(both_ref[half:, :], w_all, ((1,), (1,))).astype(low)


def columns_of(array, at, columns):
    block = at // columns
    if array.shape[1] == columns:
        return array, pl.BlockSpec(array.shape, lambda i: (0, 0))
    if at % columns:
        array = array[:, at : at + columns]
        block = 0
    return array, pl.BlockSpec((array.shape[0], columns), lambda i: (0, block))


def run_kernel(kernel, name, operands, outs, scratch=()):
    arrays, specs = [], []
    for entry in operands:
        array, spec = entry if isinstance(entry, tuple) else columns_of(entry, 0, entry.shape[1])
        arrays.append(array)
        specs.append(spec)
    return pl.pallas_call(
        kernel,
        grid=(1,),
        out_shape=[jax.ShapeDtypeStruct(shape, kind) for shape, kind in outs],
        in_specs=specs,
        out_specs=[pl.BlockSpec(shape, lambda i: (0, 0)) for shape, _ in outs],
        scratch_shapes=scratch,
        name=name,
    )(*arrays)


def forward_attention(norm_one, w_first, qk_gain, window, table, places):
    group, width = norm_one.shape[0], qk_gain.shape[1]
    square = (group, width)
    return run_kernel(
        functools.partial(attend_kernel, window),
        "attend",
        (norm_one, w_first, qk_gain, *table, *places),
        [(square, low)] * 4 + [((group, 1), full)] + [(square, full)] * 2,
    )


def forward_rest(x_own, attn_flat, weights, gain_rows, moves):
    w_outproj, w_gateup, w_down = weights
    z_one = moves.total(*moves.split(dot(attn_flat, w_outproj, ((1,), (1,)))))
    hidden = x_own + rms_scale(z_one, gain_rows[1])
    norm_three = moves.spread(rms_scale(hidden, gain_rows[2]).astype(low))
    both = dot(norm_three, w_gateup, ((1,), (0,)))
    half = both.shape[1] // 2
    act = gated(both[:, :half], both[:, half:]).astype(low)
    z_two = moves.total(*moves.split(dot(act, w_down, ((1,), (1,)))))
    result = hidden + rms_scale(z_two, gain_rows[3])
    return result, (z_one, hidden, norm_three, both, act, z_two)


def backward_ffn(weights, gain_rows, saved, back_out, moves, ready):
    z_one, hidden, norm_three, both, act, z_two = saved
    w_outproj, w_gateup, w_down = weights
    half = both.shape[1] // 2
    back_ztwo, grad_three = jax.vjp(rms_scale, z_two, gain_rows[3])[1](back_out)
    ztwo_low = moves.spread(back_ztwo.astype(low))
    back_act = dot(ztwo_low, w_down, ((1,), (0,)))
    back_gate, back_up = jax.vjp(gated, both[:, :half], both[:, half:])[1](back_act)
    both_low = jnp.concatenate([back_gate.astype(low), back_up.astype(low)], axis=1)
    back_three = moves.total(*moves.split(dot(both_low, w_gateup, ((1,), (1,)))))
    wide = [(norm_three, both_low), (ztwo_low, act)]
    if ready:
        wide, back_three = lax.optimization_barrier((outer_terms(wide), back_three))
    back_hnorm, grad_two = jax.vjp(rms_scale, hidden, gain_rows[2])[1](back_three)
    back_hidden = back_out + back_hnorm
    back_zone, grad_one = jax.vjp(rms_scale, z_one, gain_rows[1])[1](back_hidden)
    return back_hidden, back_zone, wide, (grad_one, grad_two, grad_three)


def backward_attention(x_own, norm_one, w_first, w_out, gain_rows, qk_gain, attended, back_hidden, zone_low, window, table, places, moves, outer, beside):
    q_low, k_low, v_low, mixed, logsum, qraw, kraw = attended
    group, width = qraw.shape
    model = norm_one.shape[1]
    both, own, other, grad_qk = run_kernel(
        functools.partial(attend_back_kernel, window),
        "attend_back",
        (zone_low, w_out, w_first, q_low, k_low, v_low, logsum, qraw, kraw, qk_gain, *table, *places),
        [
            ((group, 3 * width), low),
            ((group // 2, model), full),
            ((group // 2, model), low),
            ((2, width), full),
        ],
        [pltpu.VMEM((group, width), full)] * 2,
    )
    if beside is not None:
        own = beside.tie(own)
        beside.advance()
    back_one = moves.total(own, other)
    narrow = [(norm_one, both), outer]
    if beside is not None:
        back_one = beside.tie(back_one)
        narrow, back_one = lax.optimization_barrier((outer_terms(narrow), back_one))
    back_xnorm, grad_zero = jax.vjp(rms_scale, x_own, gain_rows[0])[1](back_one)
    return back_hidden + back_xnorm, narrow, grad_zero, grad_qk


def adamw(param, grad, moment, second):
    moment_new = beta_first * moment + (1.0 - beta_first) * grad
    second_new = beta_second * second + (1.0 - beta_second) * grad * grad
    moment_hat = moment_new / (1.0 - beta_first**adam_step)
    second_hat = second_new / (1.0 - beta_second**adam_step)
    updated = param - learn_rate * (
        moment_hat / (jnp.sqrt(second_hat) + adam_eps) + decay_rate * param
    )
    return (updated, moment_new, second_new)


def on_device(layer_input, positions, cotangent, *state):
    params, momenta, seconds = state[:7], state[7:14], state[14:]
    dp = lax.axis_size("dp")
    fast = tuned((dp, lax.axis_size("tensor")))
    group = positions.shape[0]
    heads_width = params[0].shape[2]
    hidden_width = params[3].shape[3]
    count_norms = params[5].shape[1]
    width = params[6].shape[2] * dp
    moves = Pairs(group) if fast else Plain(group)
    first_gather = RingGather if fast else NativeGather
    wide_scatter = WideScatter if fast else NativeScatter
    half_scatter = HalfScatter if fast else NativeScatter

    packs = [pack_layer(params, level) for level in range(2)]
    firsts = [first_gather(packs[0][0]).finish()]
    wides = [gather_native(jnp.concatenate(packs[0][1:], axis=1)), gather_native(packs[1][2])]
    first_columns = packs[0][0].shape[1]

    where_at = moves.order()
    places = moves.arrange(positions)
    marks = (where_at, places - where_at)
    marks = (jnp.stack(marks, axis=1), jnp.stack(marks, axis=0))
    windows = (WINDOW, SEQ)
    tables = [rotary_table(places, width, base) for base in rope_bases]

    current = moves.own_rows(layer_input)
    inputs, norms, attends, stores, gains, qk_gains, outs, rests = ([] for _ in range(8))
    for level in range(2):
        extra = firsts[level][:, 3 * width : first_columns]
        gain_rows, qk_gain = unpack_extra(extra, count_norms, width, dp)
        gains.append(gain_rows)
        qk_gains.append(qk_gain)
        inputs.append(current)
        norm_one = moves.spread(rms_scale(current, gain_rows[0]).astype(low))
        norms.append(norm_one)
        attended = forward_attention(
            norm_one, firsts[level], qk_gain, windows[level], tables[level], marks
        )
        if level == 0:
            block = jnp.concatenate(packs[1][:2], axis=1)
            block, mixed = lax.optimization_barrier((block, attended[3]))
            attended = (*attended[:3], mixed, *attended[4:])
            ring = first_gather(block)
            ring.advance()
            ring.advance()
            w_wide = ring.tie(wides[0])
            firsts.append(ring.finish())
            outs.append((w_wide[:, :heads_width], columns_of(w_wide, 0, heads_width)))
            w_wide = w_wide[:, heads_width:]
        else:
            w_out = firsts[1][:, first_columns:]
            outs.append((w_out, columns_of(w_out, 0, heads_width)))
            w_wide = wides[1]
        rests.append((outs[level][0], w_wide[:, : 2 * hidden_width], w_wide[:, 2 * hidden_width :]))
        attends.append(attended)
        current, store = forward_rest(current, attended[3], rests[level], gain_rows, moves)
        stores.append(store)
    top = moves.my_rows(current)

    back = moves.own_rows(cotangent)
    shards = [None, None]
    extra_grads = []
    for level in (1, 0):
        back_hidden, back_zone, wide, norm_grads = backward_ffn(
            rests[level], gains[level], stores[level], back, moves, level == 0
        )
        zone_low = moves.spread(back_zone.astype(low))
        beside = None
        if level == 0:
            beside = wide_scatter(wide)
            zone_low = beside.tie(zone_low)
            beside.advance()
        outer = (zone_low, attends[level][3])
        back, narrow, grad_zero, grad_qk = backward_attention(
            inputs[level], norms[level], firsts[level], outs[level][1], gains[level],
            qk_gains[level], attends[level], back_hidden, zone_low, windows[level],
            tables[level], marks, moves, outer, beside,
        )
        gain_grads = jnp.stack((grad_zero,) + norm_grads) * moves.weight
        extra_grads.append(pack_extra(gain_grads, grad_qk, dp))
        if level == 1:
            terms = outer_terms(narrow + wide)
            terms, back = lax.optimization_barrier((terms, back))
            sums = scatter_native(terms)
            columns = 3 * width + heads_width
            shards[1] = (sums[:, :columns], sums[:, columns:])
        else:
            slim = half_scatter(narrow)
    extra_columns = extra_grads[0].shape[1]
    extra = jnp.concatenate(extra_grads[::-1], axis=1)
    extra = half_scatter(jnp.pad(extra, ((0, 0), (0, EXTRA - 2 * extra_columns))))
    first, extra, second = run_rings([slim, extra, beside], [0, 0, 0])
    shards[0] = (first, second)
    bottom = moves.my_rows(back)

    keyvals = [first[:, heads_width : 3 * width] for first, _ in shards]
    early, _ = moves.everywhere(keyvals[1], ())
    last = jnp.concatenate([keyvals[0], extra], axis=1)
    shared, (early,) = moves.everywhere(last, (early,))
    first, second = shards[0]
    shared, second = lax.optimization_barrier((shared, second))
    shards[0] = (first, second)
    big = [
        jnp.stack([first[:, :heads_width] for first, _ in shards]),
        jnp.stack([first[:, 3 * width :].T for first, _ in shards]),
        jnp.stack(
            [
                jnp.stack([second[:, :hidden_width], second[:, hidden_width : 2 * hidden_width]])
                for _, second in shards
            ]
        ),
        jnp.stack([second[:, 2 * hidden_width :].T for _, second in shards]),
    ]
    big_results = [
        adamw(params[at], grad, momenta[at], seconds[at]) for at, grad in zip((0, 2, 3, 4), big)
    ]
    extras = [
        shared[:, 2 * width + level * extra_columns :][:, :extra_columns] for level in range(2)
    ]
    small = [
        jnp.stack([shared[:, : 2 * width], early]),
        jnp.stack([extra[:, :count_norms].T for extra in extras]),
        jnp.stack([extra[: width // dp, count_norms:].T for extra in extras]),
    ]
    small_results = [
        adamw(params[at], grad, momenta[at], seconds[at]) for at, grad in zip((1, 5, 6), small)
    ]
    gradients = (big[0], small[0], big[1], big[2], big[3], small[1], small[2])
    results = [
        big_results[0], small_results[0], *big_results[1:], small_results[1], small_results[2],
    ]
    return (
        (top, bottom)
        + gradients
        + tuple(entry[0] for entry in results)
        + tuple(entry[1] for entry in results)
        + tuple(entry[2] for entry in results)
    )


def solution(mesh):
    rows = P(("dp", "tensor"), None)
    weights = (
        P(None, "dp", "tensor"),
        P(None, "dp", None),
        P(None, "tensor", "dp"),
        P(None, None, "dp", "tensor"),
        P(None, "tensor", "dp"),
        P(None, None, "dp"),
        P(None, None, "dp"),
    )
    return jax.shard_map(
        on_device,
        mesh=mesh,
        in_specs=(rows, P("dp"), rows) + weights * 3,
        out_specs=(rows, rows) + weights * 4,
        check_vma=False,
    )
```
